768 devices in a mesh: dp: 48 (over z, y_hi), fsdp: 16 (over y_lo, x, core).
Axes of the slice: x: 4, y: 8 (y_hi: 4, y_lo: 2; y = y_hi * 2 + y_lo), z: 12, core: 2. Of those that a mesh axis runs over, the one named last changes fastest.
Arguments:
- tokens: bfloat16 [16, 48, 128, 4096], P('fsdp', 'dp'), may hold values from -6 to 6
- grad_out: bfloat16 [16, 48, 128, 4096], P('fsdp', 'dp'), may hold values from -6 to 6
- qkv_weight: bfloat16 [4096, 768], P('fsdp'), may hold values from -0.1875 to 0.1875
- out_weight: bfloat16 [4096, 512], P('fsdp'), may hold values from -0.25 to 0.25
- range_len: int32 [16, 48], P('fsdp'), may hold values from 1 to 192, 6144 in all within a row
- doc_start: int32 [16, 48, 128], P('fsdp', 'dp'), may hold values 0 or 1
Outputs:
- block_out: bfloat16 [16, 48, 128, 4096], P('fsdp', 'dp')
- tokens_grad: bfloat16 [16, 48, 128, 4096], P('fsdp', 'dp')
- qkv_grad: float32 [4096, 768], P('fsdp')
- out_grad: float32 [4096, 512], P('fsdp')
The draws below stay inside these ranges and needn't reach their ends.
Inputs may be any that keep to these rules, and one draw needn't show every extreme that they name: `range_len`: in each pack some range has exactly 192 positions.
All inputs are finite; a program needn't handle non-finite values. No bound on the sum of `doc_start` on one device may be relied on, other than what follows from the above.
Results may differ from the reference program's by a relative error of at most 0.019.
The reference program's roundings to bfloat16 on the way count: a program that leaves them out, or rounds other values in their place, can miss the bound.
Values may be sent and summed in bfloat16 or wider, within the bound.
No kernel may reach another device: no remote copies, remote signals or barrier semaphores. Data moves between devices by JAX's collectives and lax.ppermute only.
A program may use at most 64 MiB of HBM per device.

```python
import math
import jax
import jax.numpy as jnp
import numpy as np
from jax import lax

D = 4096
HS = 128
QH = 4
TOK_DEV = 128
MOST = 192
PACK = 6144
N_DP = 48
N_FSDP = 16


def draw_qkv_weight(key, part):
    key_query = jax.random.fold_in(key, 11)
    key_value = jax.random.fold_in(key, 12)
    query_part = jnp.clip(jax.random.normal(key_query, (D, QH * HS), jnp.float32), -5.0, 5.0)
    value_part = jnp.clip(jax.random.normal(key_value, (D, 2 * HS), jnp.float32), -5.0, 5.0)
    whole_draw = jnp.concatenate([query_part, value_part], axis=1)
    whole_draw = jnp.clip(whole_draw, -12.0, 12.0)
    return (whole_draw * D ** (-0.5)).astype(jnp.bfloat16)


def touch_ends(values, stream_key, least, largest):
    longest = values.shape.index(max(values.shape))
    spots = []
    for shift in (0, 1):
        where = [jax.random.randint(jax.random.fold_in(stream_key, axis), (), 0, length) for axis, length in enumerate(values.shape)]
        where[longest] = (where[longest] + shift) % values.shape[longest]
        spots.append(tuple(where))
    return values.at[spots[0]].set(least).at[spots[1]].set(largest)


def with_spikes(entries, rng, source, target, parts, factor):
    def block_of(dim):
        return (jnp.arange(entries.shape[dim]) // (entries.shape[dim] // parts)).reshape((-1,) + (1,) * (entries.ndim - 1 - dim))

    one_side = jax.random.permutation(rng, parts)[block_of(target)]
    second = (block_of(target) + parts // 2) % parts
    return jnp.where((block_of(source) == one_side) | (block_of(source) == second), factor * entries, entries)


def block_scale(key, dims, pieces, low, high):
    def one(dim, shards_of):
        heights = jax.random.uniform(jax.random.fold_in(jax.random.fold_in(key, 6), dim), (shards_of,), jnp.float32, low / len(pieces), high / len(pieces))
        return jnp.repeat(jnp.exp(heights), dims[dim] // shards_of).reshape((-1,) + (1,) * (len(dims) - dim - 1))

    loudness = one(*pieces[0])
    for cut in pieces[1:]:
        loudness = loudness * one(*cut)
    return loudness


def length_profile(number_of, total, bound, lean):
    portions = [(1 << 20) // math.isqrt(grade ** lean) + 1 for grade in range(2, number_of + 1)]
    rest, counts = total - bound - (number_of - 1), [1] * (number_of - 1)
    while rest > 0:
        movable = [i for i in range(number_of - 1) if counts[i] < bound]
        mass, remaining = sum([portions[i] for i in movable]), rest
        for i in movable:
            addition = min(bound - counts[i], max(1, remaining * portions[i] // mass), rest)
            counts[i] = counts[i] + addition
            rest = rest - addition
    return np.array([bound] + counts)


def uneven(key, count, total, limit, skew):
    if count == 2:
        one = jax.random.randint(key, (), max(1, total - limit), min(limit, total - 1) + 1)
        return jnp.stack([one, total - one])
    sizes = jnp.asarray(length_profile(count, total, limit, skew), jnp.int32)
    twos = (count - 1) // 2
    giver, receiver = sizes[1:1 + 2 * twos:2], sizes[2:2 + 2 * twos:2]
    margin = jnp.minimum(giver - 1, limit - receiver)
    shifted = jax.random.randint(jax.random.fold_in(key, 1), (twos,), 0, 1 << 20) % (margin + 1)
    sizes = sizes.at[1:1 + 2 * twos:2].set(giver - shifted).at[2:2 + 2 * twos:2].set(receiver + shifted)
    return sizes[jax.random.permutation(jax.random.fold_in(key, 2), count)]


def noise(stream_key, shape, spread, most, split=(), held_as=jnp.bfloat16):
    factor_of = block_scale(stream_key, shape, split, -0.22, 0.18) if split else 1.0
    values = jax.random.normal(stream_key, shape, jnp.float32) * spread * factor_of
    return jnp.minimum(jnp.maximum(values, -most), most).astype(held_as)


def bell_draw_with(own_key, shape, scale, reach, split, heavy, kind=jnp.bfloat16):
    entries = scale * jax.random.normal(own_key, shape, jnp.float32)
    if split:
        entries = entries * block_scale(own_key, shape, split, -0.22, 0.18)
    return jnp.clip(with_spikes(entries, jax.random.fold_in(own_key, 3), *heavy), -reach, reach).astype(kind)


def setup_inputs(seed: int = 0) -> dict:
    seeds = jax.random.split(jax.random.key(seed), 7)
    return {
        "tokens": noise(seeds[0], (N_FSDP, N_DP, TOK_DEV, D), 1.0, 6.0, ((0, 16), (1, 48))),
        "grad_out": bell_draw_with(seeds[1], (N_FSDP, N_DP, TOK_DEV, D), 1.0, 6.0, ((0, 16), (1, 48)), (0, 3, 16, 2.0)),
        "qkv_weight": draw_qkv_weight(jax.random.fold_in(seeds[6], 71), 0),
        "out_weight": noise(seeds[3], (D, QH * HS), (QH * HS) ** -0.5, 0.25, ((0, 16),)),
        "range_len": jax.vmap(lambda own: uneven(own, N_DP, PACK, MOST, 2))(jax.random.split(seeds[4], N_FSDP)).reshape((N_FSDP, N_DP)).astype(jnp.int32),
        "doc_start": touch_ends((jax.random.randint(seeds[5], (N_FSDP, N_DP, TOK_DEV), 0, 32) < 1).astype(jnp.int32), jax.random.fold_in(seeds[5], 1), 0, 1),
    }


def normalize(token_rows):
    values = token_rows.astype(jnp.float32)
    inverse = lax.rsqrt(lax.optimization_barrier(jnp.mean(values * values, axis=-1, keepdims=True)) + 1e-05)
    return (values * inverse, inverse)

def contract_rows(left, right):
    return lax.dot_general(left, right, (((0,), (0,)), ((), ())), preferred_element_type=jnp.float32)

def contract_cols(left, right):
    return lax.dot_general(left, right, (((1,), (1,)), ((), ())), preferred_element_type=jnp.float32)

def allowed_keys(position, is_live, flags):
    starts_here = (flags > 0) & is_live & (position > 0)
    before = position[None, :] <= position[:, None]
    doc_number = lax.optimization_barrier(jnp.sum((before & starts_here[None, :]).astype(jnp.int32), axis=1, dtype=jnp.int32))
    allowed = before & (doc_number[None, :] == doc_number[:, None]) & is_live[None, :] & is_live[:, None]
    return allowed | (position[None, :] == position[:, None])

def split_heads(slot_block, heads):
    head_size = slot_block.shape[1] // (heads + 2)
    rows = slot_block.shape[0]
    queries = slot_block[:, :heads * head_size].reshape(rows * heads, head_size)
    key_rows = slot_block[:, heads * head_size:(heads + 1) * head_size]
    value_rows = slot_block[:, (heads + 1) * head_size:]
    return (queries, key_rows, value_rows, head_size)

def attend_forward(slot_block, allowed, heads):
    queries, key_rows, value_rows, head_size = split_heads(slot_block, heads)
    rows = slot_block.shape[0]
    scores = contract_cols(queries, key_rows) * head_size ** (-0.5)
    scores = jnp.where(jnp.repeat(allowed, heads, axis=0), scores, -1e+30)
    row_max = lax.optimization_barrier(jnp.max(scores, axis=-1, keepdims=True))
    exponent = jnp.exp(scores - row_max)
    weights = exponent / lax.optimization_barrier(jnp.sum(exponent, axis=-1, keepdims=True))
    attended = jnp.dot(weights.astype(jnp.bfloat16), value_rows, preferred_element_type=jnp.float32).astype(jnp.bfloat16)
    return (attended.reshape(rows, heads * head_size), weights)

def attend_backward(slot_block, grad_attended, attended, weights, heads):
    queries, key_rows, value_rows, head_size = split_heads(slot_block, heads)
    rows = slot_block.shape[0]
    grad_heads = grad_attended.reshape(rows * heads, head_size)
    attended_heads = attended.reshape(rows * heads, head_size)
    grad_weights = contract_cols(grad_heads, value_rows)
    row_delta = lax.optimization_barrier(jnp.sum(grad_heads.astype(jnp.float32) * attended_heads.astype(jnp.float32), axis=-1, keepdims=True))
    grad_scores = (weights * (grad_weights - row_delta) * head_size ** (-0.5)).astype(jnp.bfloat16)
    grad_queries = jnp.dot(grad_scores, key_rows, preferred_element_type=jnp.float32).astype(jnp.bfloat16)
    grad_keys = contract_rows(grad_scores, queries).astype(jnp.bfloat16)
    grad_values = contract_rows(weights.astype(jnp.bfloat16), grad_heads).astype(jnp.bfloat16)
    return jnp.concatenate([grad_queries.reshape(rows, heads * head_size), grad_keys, grad_values], axis=1)

def to_pack(array):
    shaped = array.reshape((N_DP, TOK_DEV) + array.shape[1:])
    return jnp.swapaxes(shaped, 0, 1).reshape((N_DP * TOK_DEV,) + array.shape[1:])

def from_pack(array):
    shaped = array.reshape((TOK_DEV, N_DP) + array.shape[1:])
    return jnp.swapaxes(shaped, 0, 1).reshape((N_DP * TOK_DEV,) + array.shape[1:])

def reference(tokens, grad_out, qkv_weight, out_weight, range_len, doc_start):
    qkv_width = qkv_weight.shape[1]
    out_width = out_weight.shape[1]

    def one_pack(pack_data):
        token_rows, cot_rows, lengths, flags = pack_data
        normed, inverse = normalize(token_rows.reshape(N_DP * TOK_DEV, D))
        normed_b = normed.astype(jnp.bfloat16)
        flat_cot = cot_rows.reshape(N_DP * TOK_DEV, D)
        projected = jnp.dot(normed_b, qkv_weight, preferred_element_type=jnp.float32).astype(jnp.bfloat16)
        grad_attn = jnp.dot(flat_cot, out_weight, preferred_element_type=jnp.float32).astype(jnp.bfloat16)
        padded_qkv = jnp.concatenate([to_pack(projected), jnp.zeros((MOST, qkv_width), projected.dtype)], axis=0)
        padded_grad = jnp.concatenate([to_pack(grad_attn), jnp.zeros((MOST, out_width), grad_attn.dtype)], axis=0)
        padded_flags = jnp.concatenate([to_pack(flags.reshape(N_DP * TOK_DEV)), jnp.zeros((MOST,), jnp.int32)], axis=0)
        range_end = jnp.cumsum(lengths, dtype=jnp.int32)
        starts = range_end - lengths
        position = jnp.arange(MOST, dtype=jnp.int32)

        def range_step(range_idx, buffers):
            out_buf, grad_buf = buffers
            first_row = starts[range_idx].astype(jnp.int32)
            is_live = position < lengths[range_idx]
            slot_block = lax.dynamic_slice_in_dim(padded_qkv, first_row, MOST, 0)
            grad_block = lax.dynamic_slice_in_dim(padded_grad, first_row, MOST, 0)
            flag_block = lax.dynamic_slice_in_dim(padded_flags, first_row, MOST, 0)
            allowed = allowed_keys(position, is_live, flag_block)
            attended, weights = attend_forward(slot_block, allowed, QH)
            grad_qkv = attend_backward(slot_block, grad_block, attended, weights, QH)
            keeper = is_live[:, None]
            old_out = lax.dynamic_slice_in_dim(out_buf, first_row, MOST, 0)
            old_grad = lax.dynamic_slice_in_dim(grad_buf, first_row, MOST, 0)
            out_buf = lax.dynamic_update_slice_in_dim(out_buf, jnp.where(keeper, attended, old_out), first_row, 0)
            grad_buf = lax.dynamic_update_slice_in_dim(grad_buf, jnp.where(keeper, grad_qkv, old_grad), first_row, 0)
            return (out_buf, grad_buf)
        out_init = jnp.zeros((N_DP * TOK_DEV + MOST, out_width), projected.dtype)
        grad_init = jnp.zeros((N_DP * TOK_DEV + MOST, qkv_width), projected.dtype)
        out_buf, grad_buf = lax.fori_loop(0, N_DP, range_step, (out_init, grad_init))
        attended_rows = from_pack(out_buf[:N_DP * TOK_DEV])
        grad_rows = from_pack(grad_buf[:N_DP * TOK_DEV])
        result = token_rows.reshape(N_DP * TOK_DEV, D).astype(jnp.float32) + contract_cols(attended_rows, out_weight)
        grad_normed = contract_cols(grad_rows, qkv_weight)
        correction = lax.optimization_barrier(jnp.mean(grad_normed * normed, axis=-1, keepdims=True))
        tokens_grad = flat_cot.astype(jnp.float32) + inverse * (grad_normed - normed * correction)

        def device_step(summed, device_idx):
            first_row = (device_idx * TOK_DEV).astype(jnp.int32)
            normed_part = lax.dynamic_slice_in_dim(normed_b, first_row, TOK_DEV, 0)
            grad_part = lax.dynamic_slice_in_dim(grad_rows, first_row, TOK_DEV, 0)
            cot_part = lax.dynamic_slice_in_dim(flat_cot, first_row, TOK_DEV, 0)
            att_part = lax.dynamic_slice_in_dim(attended_rows, first_row, TOK_DEV, 0)
            partial_value = jnp.concatenate([contract_rows(normed_part, grad_part), contract_rows(cot_part, att_part)], axis=1)
            rounded = lax.optimization_barrier(partial_value.astype(jnp.bfloat16))
            return (summed + rounded.astype(jnp.float32), None)
        summed, unused = lax.scan(device_step, jnp.zeros((D, qkv_width + out_width), jnp.float32), jnp.arange(N_DP, dtype=jnp.int32))
        return (result.astype(jnp.bfloat16).reshape(N_DP, TOK_DEV, D), tokens_grad.astype(jnp.bfloat16).reshape(N_DP, TOK_DEV, D), summed)
    block_out, tokens_grad, summed = lax.map(one_pack, (tokens, grad_out, range_len, doc_start))
    total_grad = lax.optimization_barrier(jnp.sum(summed, axis=0))
    return (block_out, tokens_grad, total_grad[:, :qkv_width], total_grad[:, qkv_width:])
```

```python
import jax
import jax.numpy as jnp
from jax import lax
from jax.sharding import Mesh
from jax.sharding import PartitionSpec as P

QH = 4
DP = ("z", "yh")
FSDP = ("yl", "x", "core")


def normalize(token_rows):
    values = token_rows.astype(jnp.float32)
    inverse = lax.rsqrt(jnp.mean(values * values, axis=-1, keepdims=True) + 1e-05)
    return (values * inverse, inverse)


def contract_rows(left, right):
    return lax.dot_general(
        left, right, (((0,), (0,)), ((), ())), preferred_element_type=jnp.float32
    )


def contract_cols(left, right):
    return lax.dot_general(
        left, right, (((1,), (1,)), ((), ())), preferred_element_type=jnp.float32
    )


def allowed_keys(position, is_live, flags):
    starts_here = (flags > 0) & is_live & (position > 0)
    before = position[None, :] <= position[:, None]
    doc_number = jnp.sum((before & starts_here[None, :]).astype(jnp.int32), axis=1, dtype=jnp.int32)
    allowed = (
        before & (doc_number[None, :] == doc_number[:, None]) & is_live[None, :] & is_live[:, None]
    )
    return allowed | (position[None, :] == position[:, None])


def split_heads(slot_block, heads):
    head_size = slot_block.shape[1] // (heads + 2)
    rows = slot_block.shape[0]
    queries = slot_block[:, : heads * head_size].reshape(rows * heads, head_size)
    key_rows = slot_block[:, heads * head_size : (heads + 1) * head_size]
    value_rows = slot_block[:, (heads + 1) * head_size :]
    return (queries, key_rows, value_rows, head_size)


def attend_forward(slot_block, allowed, heads):
    queries, key_rows, value_rows, head_size = split_heads(slot_block, heads)
    rows = slot_block.shape[0]
    scores = contract_cols(queries, key_rows) * head_size ** (-0.5)
    scores = jnp.where(jnp.repeat(allowed, heads, axis=0), scores, -1e30)
    row_max = jnp.max(scores, axis=-1, keepdims=True)
    exponent = jnp.exp(scores - row_max)
    weights = exponent / jnp.sum(exponent, axis=-1, keepdims=True)
    attended = jnp.dot(
        weights.astype(jnp.bfloat16), value_rows, preferred_element_type=jnp.float32
    ).astype(jnp.bfloat16)
    return (attended.reshape(rows, heads * head_size), weights)


def attend_backward(slot_block, grad_attended, attended, weights, heads):
    queries, key_rows, value_rows, head_size = split_heads(slot_block, heads)
    rows = slot_block.shape[0]
    grad_heads = grad_attended.reshape(rows * heads, head_size)
    attended_heads = attended.reshape(rows * heads, head_size)
    grad_weights = contract_cols(grad_heads, value_rows)
    row_delta = jnp.sum(
        grad_heads.astype(jnp.float32) * attended_heads.astype(jnp.float32), axis=-1, keepdims=True
    )
    grad_scores = (weights * (grad_weights - row_delta) * head_size ** (-0.5)).astype(jnp.bfloat16)
    grad_queries = jnp.dot(grad_scores, key_rows, preferred_element_type=jnp.float32).astype(
        jnp.bfloat16
    )
    grad_keys = contract_rows(grad_scores, queries).astype(jnp.bfloat16)
    grad_values = contract_rows(weights.astype(jnp.bfloat16), grad_heads).astype(jnp.bfloat16)
    return jnp.concatenate(
        [grad_queries.reshape(rows, heads * head_size), grad_keys, grad_values], axis=1
    )


def on_device(tokens, grad_out, qkv_weight, out_weight, range_len, doc_start):
    token_rows = tokens[0, 0]
    cot_rows = grad_out[0, 0]
    flag_rows = doc_start[0, 0].astype(jnp.bfloat16)
    lengths = range_len[0]
    row_count = token_rows.shape[0]
    model_width = token_rows.shape[1]
    qkv_width = qkv_weight.shape[1]
    out_width = out_weight.shape[1]
    groups = lax.axis_size(DP)
    owners = lax.axis_size(FSDP)
    my_index = lax.axis_index(DP)
    slot_count = 3 * row_count // 2 // groups
    total_slots = groups * slot_count
    range_end = jnp.cumsum(lengths, dtype=jnp.int32)
    starts = range_end - lengths
    pack_row = my_index + groups * jnp.arange(row_count, dtype=jnp.int32)
    target = jnp.sum(
        (range_end[None, :] <= pack_row[:, None]).astype(jnp.int32), axis=1, dtype=jnp.int32
    )
    range_ids = jnp.arange(groups, dtype=jnp.int32)
    range_first = jnp.sum(
        jnp.where(range_ids[None, :] == target[:, None], starts[None, :], 0),
        axis=1,
        dtype=jnp.int32,
    )
    flat_slot = target * slot_count + (pack_row - range_first) // groups
    routing = (jnp.arange(total_slots, dtype=jnp.int32)[:, None] == flat_slot[None, :]).astype(
        jnp.bfloat16
    )

    def to_slots(array):
        placed = jnp.dot(routing, array, preferred_element_type=jnp.float32).astype(jnp.bfloat16)
        return placed.reshape((groups, slot_count) + array.shape[1:])

    def from_slots(array):
        return contract_rows(routing, array.reshape(total_slots, -1)).astype(jnp.bfloat16)

    weight_in, weight_back = (
        lax.all_gather(qkv_weight, FSDP, axis=0, tiled=True),
        lax.all_gather(out_weight, FSDP, axis=0, tiled=True),
    )
    normed, inverse = normalize(token_rows)
    normed_b = normed.astype(jnp.bfloat16)
    projected = jnp.dot(normed_b, weight_in, preferred_element_type=jnp.float32).astype(
        jnp.bfloat16
    )
    grad_attn = jnp.dot(cot_rows, weight_back, preferred_element_type=jnp.float32).astype(
        jnp.bfloat16
    )
    my_start = starts[my_index]
    my_length = lengths[my_index]
    source_ids = jnp.arange(groups, dtype=jnp.int32)[:, None]
    slot_ids = jnp.arange(slot_count, dtype=jnp.int32)[None, :]
    position = ((source_ids - my_start) % groups + groups * slot_ids).reshape(total_slots)
    is_live = position < my_length
    got_flags = swap_dp(to_slots(flag_rows))
    got_qkv = swap_dp(to_slots(projected))
    allowed = allowed_keys(position, is_live, got_flags.reshape(total_slots))
    slot_block = got_qkv.reshape(total_slots, qkv_width)
    attended, weights = attend_forward(slot_block, allowed, QH)
    got_grad = swap_dp(to_slots(grad_attn))
    grad_block = attend_backward(
        slot_block, got_grad.reshape(total_slots, out_width), attended, weights, QH
    )
    both = jnp.concatenate([grad_block, attended], axis=1)
    back = swap_dp(both.reshape(groups, slot_count, qkv_width + out_width))
    both_rows = from_slots(back)
    grad_rows = both_rows[:, :qkv_width]
    attended_rows = both_rows[:, qkv_width:]
    result = (token_rows.astype(jnp.float32) + contract_cols(attended_rows, weight_back)).astype(
        jnp.bfloat16
    )
    grad_normed = contract_cols(grad_rows, weight_in)
    correction = jnp.mean(grad_normed * normed, axis=-1, keepdims=True)
    tokens_grad = (
        cot_rows.astype(jnp.float32) + inverse * (grad_normed - normed * correction)
    ).astype(jnp.bfloat16)
    normed_cols, cot_cols = (
        lax.all_to_all(normed_b, FSDP, split_axis=1, concat_axis=0, tiled=True),
        lax.all_to_all(cot_rows, FSDP, split_axis=1, concat_axis=0, tiled=True),
    )
    both_all = lax.all_gather(both_rows, FSDP, axis=0, tiled=True)
    partial = jnp.concatenate(
        [
            contract_rows(normed_cols, both_all[:, :qkv_width]),
            contract_rows(cot_cols, both_all[:, qkv_width:]),
        ],
        axis=1,
    ).astype(jnp.bfloat16)
    summed = sum_over_dp(partial, groups)
    return (
        result[None, None],
        tokens_grad[None, None],
        summed[:, :qkv_width],
        summed[:, qkv_width:],
    )


def swap_dp(array):
    return lax.all_to_all(array, DP, split_axis=0, concat_axis=0, tiled=True)


def sum_over_dp(partial, groups):
    rows, cols = partial.shape
    tiles = (rows // 8) * (cols // 128)
    each = -(-tiles // groups)
    tiled = jnp.swapaxes(partial.reshape(rows // 8, 8, cols // 128, 128), 1, 2)
    tiled = tiled.reshape(tiles, 8, 128)
    tiled = jnp.pad(tiled, ((0, groups * each - tiles), (0, 0), (0, 0)))
    got = swap_dp(tiled.reshape(groups, each, 8, 128))
    mine = jnp.sum(got.astype(jnp.float32), axis=0).astype(jnp.bfloat16)
    whole = lax.all_gather(mine, "yh", axis=0, tiled=True)
    whole = lax.all_gather(whole, "z", axis=0, tiled=True)[:tiles]
    whole = jnp.swapaxes(whole.reshape(rows // 8, cols // 128, 8, 128), 1, 2)
    return whole.reshape(rows, cols).astype(jnp.float32)


def solution(mesh):
    fine = Mesh(mesh.devices.reshape(12, 4, 2, 4, 2), DP + FSDP)
    return jax.shard_map(
        on_device,
        mesh=fine,
        in_specs=(
            P(FSDP, DP, None, None),
            P(FSDP, DP, None, None),
            P(FSDP, None),
            P(FSDP, None),
            P(FSDP, None),
            P(FSDP, DP, None),
        ),
        out_specs=(
            P(FSDP, DP, None, None),
            P(FSDP, DP, None, None),
            P(FSDP, None),
            P(FSDP, None),
        ),
        check_vma=False,
    )
```

```python
import functools

import jax
import jax.numpy as jnp
from jax import lax
from jax.experimental import pallas as pl
from jax.experimental.pallas import tpu as pltpu
from jax.sharding import Mesh
from jax.sharding import PartitionSpec as P


QH = 4
DP = ("z", "yh")
FINE = (12, 4, 2, 4, 2)
FSDP = ("yl", "x", "core")


def prepare_kernel(places, tokens, cot, normed, keep, send):
    width = tokens.shape[1]
    share = keep.shape[3] // 2
    values = tokens[...].astype(jnp.float32)
    squares = jnp.sum(values * values, axis=-1, keepdims=True)
    normed[...] = (values * lax.rsqrt(squares / width + 1e-05)).astype(jnp.bfloat16)
    number = 0
    for out in (keep, send):
        for dy in range(out.shape[0]):
            for dx in range(out.shape[1]):
                columns = pl.ds(pl.multiple_of(places[number] * share, 128), share)
                out[dy, dx, :, :share] = normed[:, columns]
                out[dy, dx, :, share:] = cot[:, columns]
                number += 1


def contract_rows(left, right):
    return lax.dot_general(
        left, right, (((0,), (0,)), ((), ())), preferred_element_type=jnp.float32
    )


def contract_cols(left, right):
    return lax.dot_general(
        left, right, (((1,), (1,)), ((), ())), preferred_element_type=jnp.float32
    )


def attention_kernel(heads, length, place_col, place_row, got, out):
    size = got.shape[1] // (2 * heads + 3)
    wide = heads * size
    keys = got[:, wide : wide + size]
    values = got[:, wide + size : wide + 2 * size]
    flags = got[:, 2 * wide + 2 * size :].astype(jnp.float32)
    at_col, at_row = (place_col[...], place_row[...])
    live_col, live_row = (at_col < length[0], at_row < length[0])
    begin_col = (flags[:, :1] > 0) & live_col & (at_col > 0)
    begin_row = (flags.T[:1, :] > 0) & live_row & (at_row > 0)
    before = at_row <= at_col
    after = at_col <= at_row
    count_col = jnp.sum(jnp.where(before & begin_row, 1.0, 0.0), axis=1, keepdims=True)
    count_row = jnp.sum(jnp.where(after & begin_col, 1.0, 0.0), axis=0, keepdims=True)
    allowed = (before & (count_col == count_row) & live_col & live_row) | (at_row == at_col)
    scale = size ** (-0.5)
    grad_keys, grad_values = (0.0, 0.0)
    for head in range(heads):
        columns = slice(head * size, (head + 1) * size)
        queries = got[:, columns]
        grads = got[:, wide + 2 * size + head * size : wide + 2 * size + (head + 1) * size]
        scores = jnp.where(allowed, contract_cols(queries, keys) * scale, -1e30)
        exponent = jnp.exp(scores - jnp.max(scores, axis=-1, keepdims=True))
        weights = exponent / jnp.sum(exponent, axis=-1, keepdims=True)
        weights_b = weights.astype(jnp.bfloat16)
        attended = jnp.dot(weights_b, values, preferred_element_type=jnp.float32)
        attended = attended.astype(jnp.bfloat16)
        delta = jnp.sum(
            grads.astype(jnp.float32) * attended.astype(jnp.float32), axis=-1, keepdims=True
        )
        grad_scores = weights * (contract_cols(grads, values) - delta) * scale
        grad_scores = grad_scores.astype(jnp.bfloat16)
        out[:, columns] = jnp.dot(
            grad_scores, keys, preferred_element_type=jnp.float32
        ).astype(jnp.bfloat16)
        grad_keys += contract_rows(grad_scores, queries)
        grad_values += contract_rows(weights_b, grads)
        shifted = slice(wide + 2 * size + head * size, wide + 2 * size + (head + 1) * size)
        out[:, shifted] = attended
    out[:, wide : wide + size] = grad_keys.astype(jnp.bfloat16)
    out[:, wide + size : wide + 2 * size] = grad_values.astype(jnp.bfloat16)


def spread_kernel(split, whole, first, second):
    share = first.shape[0]
    for at in range(0, first.shape[1] + second.shape[1], 128):
        piece = whole[at // 128 * share : at // 128 * share + share, :].astype(jnp.float32)
        if at < split:
            first[:, at : at + 128] = piece
        else:
            second[:, at - split : at - split + 128] = piece


def shift_x(array, step):
    size = lax.axis_size("x")
    return lax.ppermute(array, "x", [(i, (i + step) % size) for i in range(size)])


def shift_y(array, step):
    size = lax.axis_size(("yh", "yl"))
    return lax.ppermute(array, ("yh", "yl"), [(i, (i + step) % size) for i in range(size)])


def swap_y(array):
    return lax.ppermute(array, "yl", [(0, 1), (1, 0)])


def swap_core(array):
    return lax.ppermute(array, "core", [(0, 1), (1, 0)])


def place(dx, dy, dc):
    yl = (lax.axis_index("yl") + dy) % 2
    x = (lax.axis_index("x") + dx) % lax.axis_size("x")
    core = (lax.axis_index("core") + dc) % 2
    return ((yl * lax.axis_size("x") + x) * 2 + core).astype(jnp.int32)


def label_blocks(groups):
    arrays, pieces, places = [], [], []
    for dc, array, parts in groups:
        row = 0
        for dx, dy, sub, rows in parts:
            pieces.append((len(arrays), row, sub, rows))
            places.append((dx % 4, dy, dc))
            row += rows
        arrays.append(array)
    return (arrays, pieces, places)


def place_all(offsets):
    return jnp.stack([place(*offset) for offset in offsets])


def spread_cols(keep, send):
    other = swap_core(send)
    across_0 = swap_y(keep[1])
    across_1 = swap_y(other[1])
    return (keep[0], other[0], across_0, across_1)


def spread_cols_x(here):
    quads = [[part[dx] for part in here] for dx in range(4)]
    up = jnp.stack(quads[1] + quads[2][:2])
    down = jnp.stack(quads[3] + quads[2][2:])
    up = shift_x(up, 1)
    down = shift_x(down, -1)
    far_up = shift_x(up[4:], 1)
    far_down = shift_x(down[4:], -1)
    sources = [(0, 0), (0, 1), (1, 0), (1, 1)]
    arrays = [*here, up, down, far_up, far_down]
    pieces = [(number, 0, (0, *source)) for number, source in enumerate(sources)]
    pieces += [(4, number, (3, *source)) for number, source in enumerate(sources)]
    pieces += [(5, number, (1, *source)) for number, source in enumerate(sources)]
    pieces += [(6, number, (2, *source)) for number, source in enumerate(sources[:2])]
    pieces += [(7, number, (2, *source)) for number, source in enumerate(sources[2:])]
    return (arrays, pieces)


def gather_weights(block, beside):
    half = block.shape[0] // 2
    full = 2 * half
    left = shift_x(block, 1)
    right = shift_x(block, -1)
    across_a = shift_y(block[:half], 1)
    across_b = shift_y(block[half:], -1)
    other_0 = swap_core(block)
    left, right, across_a, across_b, other_0, beside = lax.optimization_barrier(
        (left, right, across_a, across_b, other_0, beside)
    )
    left_y = shift_y(left, 1)
    right_y = shift_y(right, -1)
    far_a = shift_x(left[:half], 1)
    far_b = shift_x(right[half:], -1)
    other_1 = swap_core(jnp.concatenate([left, right, across_a, across_b], axis=0))
    far_y_a = shift_y(far_a, 1)
    far_y_b = shift_y(far_b, -1)
    other_2 = swap_core(jnp.concatenate([left_y, right_y, far_a, far_b], axis=0))
    other_3 = swap_core(jnp.concatenate([far_y_a, far_y_b], axis=0))
    parts_1 = [(-1, 0, 0, full), (1, 0, 0, full), (0, 1, 0, half), (0, 1, half, half)]
    parts_2 = [(-1, 1, 0, full), (1, 1, 0, full), (2, 0, 0, half), (2, 0, half, half)]
    parts_3 = [(2, 1, 0, half), (2, 1, half, half)]
    mine = [block, left, right, across_a, across_b, left_y, right_y, far_a, far_b]
    mine += [far_y_a, far_y_b]
    own_parts = [(0, 0, 0, full)] + parts_1 + parts_2 + parts_3
    groups = [(0, array, [part]) for array, part in zip(mine, own_parts)]
    groups += [
        (1, other_0, [(0, 0, 0, full)]),
        (1, other_1, parts_1),
        (1, other_2, parts_2),
        (1, other_3, parts_3),
    ]
    return (*label_blocks(groups), beside)


def gather_rows(block):
    half = block.shape[0] // 2
    full = 2 * half
    left = shift_x(block, 1)
    right = shift_x(block, -1)
    across = swap_y(block)
    other_0 = swap_core(block)
    right_y = swap_y(right)
    left_y = shift_x(across, 1)
    far = shift_x(right, -1)
    other_1 = swap_core(jnp.concatenate([left, right, across], axis=0))
    far_y_a = swap_y(far[:half])
    far_y_b = shift_x(left_y[half:], 1)
    other_2 = swap_core(jnp.concatenate([right_y, left_y, far], axis=0))
    other_3 = swap_core(jnp.concatenate([far_y_a, far_y_b], axis=0))
    parts_1 = [(-1, 0, 0, full), (1, 0, 0, full), (0, 1, 0, full)]
    parts_2 = [(1, 1, 0, full), (-1, 1, 0, full), (2, 0, 0, full)]
    parts_3 = [(2, 1, 0, half), (2, 1, half, half)]
    mine = [block, left, right, across, right_y, left_y, far, far_y_a, far_y_b]
    own_parts = [(0, 0, 0, full)] + parts_1 + parts_2 + parts_3
    groups = [(0, array, [part]) for array, part in zip(mine, own_parts)]
    groups += [
        (1, other_0, [(0, 0, 0, full)]),
        (1, other_1, parts_1),
        (1, other_2, parts_2),
        (1, other_3, parts_3),
    ]
    return label_blocks(groups)


def project_kernel(pieces, share, split, places, normed, cot, routing, flags, *refs):
    blocks, (out, total) = (refs[:-2], refs[-2:])
    for number, (which, row, sub, rows) in enumerate(pieces):
        columns = pl.ds(pl.multiple_of(places[number] * share + sub, 128), rows)
        first = jnp.dot(
            normed[:, columns],
            blocks[which][row : row + rows, :split],
            preferred_element_type=jnp.float32,
        )
        second = jnp.dot(
            cot[:, columns],
            blocks[which][row : row + rows, split:],
            preferred_element_type=jnp.float32,
        )
        if number == 0:
            total[:, :split] = first
            total[:, split:] = second
        else:
            total[:, :split] += first
            total[:, split:] += second
    width = total.shape[1]
    out[:, :width] = jnp.dot(
        routing[...], total[...].astype(jnp.bfloat16), preferred_element_type=jnp.float32
    ).astype(jnp.bfloat16)
    out[:, width:] = jnp.dot(
        routing[...], flags[...], preferred_element_type=jnp.float32
    ).astype(jnp.bfloat16)


def finish_kernel(pieces, share, split, places, both, tokens, cot, *refs):
    blocks, (result, grad, back) = (refs[:-3], refs[-3:])
    grad_rows = both[:, :split]
    attended = both[:, split:]
    rows_cols = (((1,), (1,)), ((), ()))
    for number, (which, row, sub, rows) in enumerate(pieces):
        columns = pl.ds(pl.multiple_of(places[number] * share + sub, 128), rows)
        back[:, columns] = lax.dot_general(
            grad_rows,
            blocks[which][row : row + rows, :split],
            rows_cols,
            preferred_element_type=jnp.float32,
        )
        added = lax.dot_general(
            attended,
            blocks[which][row : row + rows, split:],
            rows_cols,
            preferred_element_type=jnp.float32,
        )
        result[:, columns] = (tokens[:, columns].astype(jnp.float32) + added).astype(jnp.bfloat16)
    width = tokens.shape[1]
    values = tokens[...].astype(jnp.float32)
    squares = jnp.sum(values * values, axis=-1, keepdims=True)
    inverse = lax.rsqrt(squares / width + 1e-05)
    normed = values * inverse
    correction = jnp.sum(back[...] * normed, axis=-1, keepdims=True) / width
    grad[...] = (
        cot[...].astype(jnp.float32) + inverse * (back[...] - normed * correction)
    ).astype(jnp.bfloat16)


def weight_grad_kernel(row_pieces, col_pieces, split, *refs):
    inputs, (out, rows_all, cols_all) = (refs[:-3], refs[-3:])
    col_count = 1 + max(which for which, _, _ in col_pieces)
    share = cols_all.shape[1] // 2
    count = inputs[0].shape[1]
    for which, index, to in col_pieces:
        cols_all[to : to + count, :] = inputs[which][index]
    for which, row, to, rows in row_pieces:
        rows_all[to : to + rows, :] = inputs[col_count + which][row : row + rows, :]
    first = contract_rows(cols_all[:, :share], rows_all[:, :split]).astype(jnp.bfloat16)
    second = contract_rows(cols_all[:, share:], rows_all[:, split:]).astype(jnp.bfloat16)
    step = 128
    width = rows_all.shape[1]
    for at in range(0, width, step):
        piece = first[:, at : at + step] if at < split else second[:, at - split : at - split + step]
        out[at // step * share : at // step * share + share, :] = piece
    filled = width // step * share
    if filled < out.shape[0]:
        out[filled:, :] = jnp.zeros((out.shape[0] - filled, step), jnp.bfloat16)


def call(kernel, places, operands, out_shape, scratch, flops, read):
    vmem = pl.BlockSpec(memory_space=pltpu.VMEM)
    smem = [] if places is None else [pl.BlockSpec(memory_space=pltpu.SMEM)]
    return pl.pallas_call(
        kernel,
        out_shape=out_shape,
        in_specs=smem + [vmem] * len(operands),
        out_specs=jax.tree.map(lambda _: vmem, out_shape),
        scratch_shapes=scratch,
        cost_estimate=pl.CostEstimate(flops=flops, bytes_accessed=read, transcendentals=0),
    )(*([] if places is None else [places]), *operands)


def on_device(tokens, grad_out, qkv_weight, out_weight, range_len, doc_start):
    token_rows = tokens[0, 0]
    cot_rows = grad_out[0, 0]
    flag_rows = doc_start[0, 0].astype(jnp.bfloat16)
    lengths = range_len[0]
    row_count = token_rows.shape[0]
    model_width = token_rows.shape[1]
    qkv_width = qkv_weight.shape[1]
    out_width = out_weight.shape[1]
    groups = lax.axis_size(DP)
    owners = lax.axis_size(FSDP)
    my_index = lax.axis_index(DP)
    slot_count = 3 * row_count // 2 // groups
    total_slots = groups * slot_count
    range_end = jnp.cumsum(lengths, dtype=jnp.int32)
    starts = range_end - lengths
    pack_row = my_index + groups * jnp.arange(row_count, dtype=jnp.int32)
    target = jnp.sum(
        (range_end[None, :] <= pack_row[:, None]).astype(jnp.int32), axis=1, dtype=jnp.int32
    )
    range_ids = jnp.arange(groups, dtype=jnp.int32)
    range_first = jnp.sum(
        jnp.where(range_ids[None, :] == target[:, None], starts[None, :], 0),
        axis=1,
        dtype=jnp.int32,
    )
    flat_slot = target * slot_count + (pack_row - range_first) // groups
    routing = (jnp.arange(total_slots, dtype=jnp.int32)[:, None] == flat_slot[None, :]).astype(
        jnp.bfloat16
    )

    def from_slots(array):
        return contract_rows(routing, array.reshape(total_slots, -1)).astype(jnp.bfloat16)

    width = qkv_width + out_width
    share = model_width // owners
    order = [(dx, dy, dc) for dc in range(2) for dy in range(2) for dx in range(4)]
    piece = jax.ShapeDtypeStruct((2, 4, row_count, 2 * share), jnp.bfloat16)
    normed_b, keep, send = call(
        prepare_kernel,
        place_all(order),
        [token_rows, cot_rows],
        [jax.ShapeDtypeStruct((row_count, model_width), jnp.bfloat16), piece, piece],
        [],
        4 * row_count * model_width,
        10 * row_count * model_width,
    )
    flag_cols = jnp.broadcast_to(flag_rows[:, None], (row_count, 128))
    my_start = starts[my_index]
    my_length = lengths[my_index]
    source_ids = jnp.arange(groups, dtype=jnp.int32)[:, None]
    slot_ids = jnp.arange(slot_count, dtype=jnp.int32)[None, :]
    position = ((source_ids - my_start) % groups + groups * slot_ids).reshape(total_slots)
    blocks, pieces, offsets, beside = gather_weights(
        jnp.concatenate([qkv_weight, out_weight], axis=1),
        (normed_b, keep, send, flag_cols, routing, position),
    )
    normed_b, keep, send, flag_cols, routing, position = beside
    places = place_all(offsets)
    slots = call(
        functools.partial(project_kernel, pieces, share, qkv_width),
        places,
        [normed_b, cot_rows, routing, flag_cols, *blocks],
        jax.ShapeDtypeStruct((total_slots, width + 128), jnp.bfloat16),
        [pltpu.VMEM((row_count, width), jnp.float32)],
        2 * row_count * model_width * width,
        2 * model_width * width,
    )
    slots, keep, send = lax.optimization_barrier((slots, keep, send))
    got = swap_dp(slots.reshape(groups, slot_count, width + 128))
    here = spread_cols(keep, send)
    got = got.reshape(total_slots, width + 128)
    both = call(
        functools.partial(attention_kernel, QH),
        my_length[None],
        [position[:, None], position[None, :], got],
        jax.ShapeDtypeStruct((total_slots, width), jnp.bfloat16),
        [],
        18 * total_slots * total_slots * out_width,
        4 * total_slots * width,
    )
    both, here = lax.optimization_barrier((both, here))
    back = swap_dp(both.reshape(groups, slot_count, width))
    cols, col_pieces = spread_cols_x(here)
    back, cols = lax.optimization_barrier((back, cols))
    both_rows = from_slots(back)
    row_blocks, row_pieces, row_offsets = gather_rows(both_rows)
    at = {offset: number * row_count for number, offset in enumerate(order)}
    row_pieces = [
        (which, row, at[offset] + sub, rows)
        for (which, row, sub, rows), offset in zip(row_pieces, row_offsets)
    ]
    col_pieces = [(which, index, at[offset]) for which, index, offset in col_pieces]
    each = -(-share * width // (128 * 8 * groups)) * 8
    partial = call(
        functools.partial(weight_grad_kernel, row_pieces, col_pieces, qkv_width),
        None,
        [*cols, *row_blocks],
        jax.ShapeDtypeStruct((groups * each, 128), jnp.bfloat16),
        [
            pltpu.VMEM((owners * row_count, width), jnp.bfloat16),
            pltpu.VMEM((owners * row_count, 2 * share), jnp.bfloat16),
        ],
        2 * owners * row_count * width * share,
        2 * owners * row_count * (width + 2 * share),
    )
    partial, both_late = lax.optimization_barrier((partial, both_rows))
    summed = sum_over_dp(partial.reshape(groups, each, 128))
    result, tokens_grad = call(
        functools.partial(finish_kernel, pieces, share, qkv_width),
        places,
        [both_late, token_rows, cot_rows, *blocks],
        [jax.ShapeDtypeStruct((row_count, model_width), jnp.bfloat16)] * 2,
        [pltpu.VMEM((row_count, model_width), jnp.float32)],
        2 * row_count * model_width * width,
        2 * model_width * width,
    )

    qkv_grad, out_grad = call(
        functools.partial(spread_kernel, qkv_width),
        None,
        [summed],
        [
            jax.ShapeDtypeStruct((share, qkv_width), jnp.float32),
            jax.ShapeDtypeStruct((share, out_width), jnp.float32),
        ],
        [],
        share * width,
        6 * share * width,
    )
    return (result[None, None], tokens_grad[None, None], qkv_grad, out_grad)


def swap_dp(array):
    return lax.all_to_all(array, DP, split_axis=0, concat_axis=0, tiled=True)


def sum_over_dp(partial):
    groups, each, lanes = partial.shape
    rows, cols = (lax.axis_size("z"), lax.axis_size("yh"))
    ordered = jnp.swapaxes(partial.reshape(cols, rows, each, lanes), 0, 1)
    got = swap_dp(ordered.reshape(groups, each, lanes))
    mine = jnp.sum(got.astype(jnp.float32), axis=0).astype(jnp.bfloat16)
    whole = lax.all_gather(mine, "z", axis=0, tiled=True)
    return lax.all_gather(whole, "yh", axis=0, tiled=True)


def solution(mesh):
    fine = Mesh(mesh.devices.reshape(FINE), DP + FSDP)
    return jax.shard_map(
        on_device,
        mesh=fine,
        in_specs=(
            P(FSDP, DP, None, None),
            P(FSDP, DP, None, None),
            P(FSDP, None),
            P(FSDP, None),
            P(FSDP, None),
            P(FSDP, DP, None),
        ),
        out_specs=(
            P(FSDP, DP, None, None),
            P(FSDP, DP, None, None),
            P(FSDP, None),
            P(FSDP, None),
        ),
        check_vma=False,
    )
```

```python
import functools

import jax
import jax.numpy as jnp
from jax import lax
from jax.experimental import pallas as pl
from jax.experimental.pallas import tpu as pltpu
from jax.sharding import Mesh
from jax.sharding import PartitionSpec as P


QH = 4
DP = ("z", "yh")
FINE = (12, 4, 2, 4, 2)
FSDP = ("yl", "x", "core")


def prepare_kernel(places, tokens, cot, normed, keep, send):
    width = tokens.shape[1]
    share = keep.shape[3] // 2
    values = tokens[...].astype(jnp.float32)
    squares = jnp.sum(values * values, axis=-1, keepdims=True)
    normed[...] = (values * lax.rsqrt(squares / width + 1e-05)).astype(jnp.bfloat16)
    number = 0
    for out in (keep, send):
        for dy in range(out.shape[0]):
            for dx in range(out.shape[1]):
                columns = pl.ds(pl.multiple_of(places[number] * share, 128), share)
                out[dy, dx, :, :share] = normed[:, columns]
                out[dy, dx, :, share:] = cot[:, columns]
                number += 1


def contract_rows(left, right):
    return lax.dot_general(
        left, right, (((0,), (0,)), ((), ())), preferred_element_type=jnp.float32
    )


def contract_cols(left, right):
    return lax.dot_general(
        left, right, (((1,), (1,)), ((), ())), preferred_element_type=jnp.float32
    )


def attention_kernel(heads, length, place_col, place_row, got, out):
    size = got.shape[1] // (2 * heads + 3)
    wide = heads * size
    keys = got[:, wide : wide + size]
    values = got[:, wide + size : wide + 2 * size]
    flags = got[:, 2 * wide + 2 * size :].astype(jnp.float32)
    at_col, at_row = (place_col[...], place_row[...])
    live_col, live_row = (at_col < length[0], at_row < length[0])
    begin_col = (flags[:, :1] > 0) & live_col & (at_col > 0)
    begin_row = (flags.T[:1, :] > 0) & live_row & (at_row > 0)
    before = at_row <= at_col
    after = at_col <= at_row
    count_col = jnp.sum(jnp.where(before & begin_row, 1.0, 0.0), axis=1, keepdims=True)
    count_row = jnp.sum(jnp.where(after & begin_col, 1.0, 0.0), axis=0, keepdims=True)
    allowed = (before & (count_col == count_row) & live_col & live_row) | (at_row == at_col)
    scale = size ** (-0.5)
    grad_keys, grad_values = (0.0, 0.0)
    for head in range(heads):
        columns = slice(head * size, (head + 1) * size)
        queries = got[:, columns]
        grads = got[:, wide + 2 * size + head * size : wide + 2 * size + (head + 1) * size]
        scores = jnp.where(allowed, contract_cols(queries, keys) * scale, -1e30)
        exponent = jnp.exp(scores - jnp.max(scores, axis=-1, keepdims=True))
        weights = exponent / jnp.sum(exponent, axis=-1, keepdims=True)
        weights_b = weights.astype(jnp.bfloat16)
        attended = jnp.dot(weights_b, values, preferred_element_type=jnp.float32)
        attended = attended.astype(jnp.bfloat16)
        delta = jnp.sum(
            grads.astype(jnp.float32) * attended.astype(jnp.float32), axis=-1, keepdims=True
        )
        grad_scores = weights * (contract_cols(grads, values) - delta) * scale
        grad_scores = grad_scores.astype(jnp.bfloat16)
        out[:, columns] = jnp.dot(
            grad_scores, keys, preferred_element_type=jnp.float32
        ).astype(jnp.bfloat16)
        grad_keys += contract_rows(grad_scores, queries)
        grad_values += contract_rows(weights_b, grads)
        shifted = slice(wide + 2 * size + head * size, wide + 2 * size + (head + 1) * size)
        out[:, shifted] = attended
    out[:, wide : wide + size] = grad_keys.astype(jnp.bfloat16)
    out[:, wide + size : wide + 2 * size] = grad_values.astype(jnp.bfloat16)


def spread_kernel(split, whole, first, second):
    share = first.shape[0]
    for at in range(0, first.shape[1] + second.shape[1], 128):
        piece = whole[at // 128 * share : at // 128 * share + share, :].astype(jnp.float32)
        if at < split:
            first[:, at : at + 128] = piece
        else:
            second[:, at - split : at - split + 128] = piece


def shift_x(array, step):
    size = lax.axis_size("x")
    return lax.ppermute(array, "x", [(i, (i + step) % size) for i in range(size)])


def along_x(array):
    size = lax.axis_size("x")
    pairs = []
    for i in range(size):
        pairs.append((2 * i, (i + 1) % size * 2))
        pairs.append((2 * i + 1, (i - 1) % size * 2 + 1))
    return lax.ppermute(array, ("x", "core"), pairs)


def along_y(array):
    size = lax.axis_size(("yh", "yl"))
    pairs = []
    for i in range(size):
        pairs.append((2 * i, (i + 1) % size * 2))
        pairs.append((2 * i + 1, (i - 1) % size * 2 + 1))
    return lax.ppermute(array, ("yh", "yl", "core"), pairs)


def swap_y(array):
    return lax.ppermute(array, "yl", [(0, 1), (1, 0)])


def swap_core(array):
    return lax.ppermute(array, "core", [(0, 1), (1, 0)])


def place(dx, dy, dc):
    yl = (lax.axis_index("yl") + dy) % 2
    x = (lax.axis_index("x") + dx) % lax.axis_size("x")
    core = (lax.axis_index("core") + dc) % 2
    return ((yl * lax.axis_size("x") + x) * 2 + core).astype(jnp.int32)


def label_blocks(groups):
    arrays, pieces, places = [], [], []
    for dc, array, parts in groups:
        row = 0
        for dx, dy, sub, rows in parts:
            pieces.append((len(arrays), row, sub, rows))
            places.append((dx % 4, dy, dc))
            row += rows
        arrays.append(array)
    return (arrays, pieces, places)


def place_all(offsets):
    return jnp.stack([place(*offset) for offset in offsets])


def pack_kernel(keep, other, across, up, down):
    half = across.shape[0] // 2
    for out, dx, tail in ((up, 1, (keep[0, 2], other[0, 2])), (down, 3, (across[2], across[half + 2]))):
        out[0] = keep[0, dx]
        out[1] = other[0, dx]
        out[2] = across[dx]
        out[3] = across[half + dx]
        out[4] = tail[0]
        out[5] = tail[1]


def spread_cols(keep, other, ahead):
    piece = keep.shape[2:]
    across = swap_y(ahead)
    up, down = call(
        pack_kernel,
        None,
        [keep, other, across],
        [jax.ShapeDtypeStruct((6, *piece), jnp.bfloat16)] * 2,
        [],
        keep.size,
        12 * keep.size,
    )
    up = shift_x(up, 1)
    down = shift_x(down, -1)
    far_up = shift_x(up[4:], 1)
    far_down = shift_x(down[4:], -1)
    sources = [(0, 0), (0, 1), (1, 0), (1, 1)]
    arrays = [keep, other, across, up, down, far_up, far_down]
    pieces = [(0, (0, 0), (0, 0, 0)), (1, (0, 0), (0, 0, 1))]
    pieces += [(2, (0,), (0, 1, 0)), (2, (4,), (0, 1, 1))]
    pieces += [(3, (number,), (3, *source)) for number, source in enumerate(sources)]
    pieces += [(4, (number,), (1, *source)) for number, source in enumerate(sources)]
    pieces += [(5, (number,), (2, *source)) for number, source in enumerate(sources[:2])]
    pieces += [(6, (number,), (2, *source)) for number, source in enumerate(sources[2:])]
    return (arrays, pieces)


def gather_weights(block, first_dot, beside):
    rows = block.shape[0]
    sign = 1 - 2 * lax.axis_index("core")
    other_0 = swap_core(block)
    across = along_y(block)
    chip = jnp.concatenate([block, other_0], axis=0)
    side = along_x(chip)
    side, across, beside = lax.optimization_barrier((side, across, beside))
    side_y = along_y(side)
    far = along_x(side[:rows])
    other_1 = swap_core(jnp.concatenate([side, across], axis=0))
    groups = [
        (block, [(0, 0, 0)]),
        (other_0, [(0, 0, 1)]),
        (side, [(-sign, 0, 0), (-sign, 0, 1)]),
        (across, [(0, 1, 0)]),
        (other_1, [(sign, 0, 1), (sign, 0, 0), (0, 1, 1)]),
    ]
    early = number_blocks(groups, rows)
    total = first_dot(beside, *early)
    far, total = lax.optimization_barrier((far, total))
    far_y = along_y(far)
    other_2 = swap_core(jnp.concatenate([side_y, far], axis=0))
    other_3 = swap_core(far_y)
    groups = [
        (side_y, [(-sign, 1, 0), (-sign, 1, 1)]),
        (far, [(2, 0, 0)]),
        (far_y, [(2, 1, 0)]),
        (other_2, [(sign, 1, 1), (sign, 1, 0), (2, 0, 1)]),
        (other_3, [(2, 1, 1)]),
    ]
    return (early, number_blocks(groups, rows), total, beside)


def number_blocks(groups, rows):
    arrays, pieces, places = [], [], []
    for array, offsets in groups:
        for number, offset in enumerate(offsets):
            pieces.append((len(arrays), number * rows, 0, rows))
            places.append(place(*offset))
        arrays.append(array)
    return (arrays, pieces, jnp.stack(places))


def gather_rows(block):
    half = block.shape[0] // 2
    full = 2 * half
    left = shift_x(block, 1)
    right = shift_x(block, -1)
    across = swap_y(block)
    other_0 = swap_core(block)
    right_y = swap_y(right)
    left_y = shift_x(across, 1)
    far = shift_x(right, -1)
    other_1 = swap_core(jnp.concatenate([left, right, across], axis=0))
    far_y_a = swap_y(far[:half])
    far_y_b = shift_x(left_y[half:], 1)
    other_2 = swap_core(jnp.concatenate([right_y, left_y, far], axis=0))
    other_3 = swap_core(jnp.concatenate([far_y_a, far_y_b], axis=0))
    parts_1 = [(-1, 0, 0, full), (1, 0, 0, full), (0, 1, 0, full)]
    parts_2 = [(1, 1, 0, full), (-1, 1, 0, full), (2, 0, 0, full)]
    parts_3 = [(2, 1, 0, half), (2, 1, half, half)]
    mine = [block, left, right, across, right_y, left_y, far, far_y_a, far_y_b]
    own_parts = [(0, 0, 0, full)] + parts_1 + parts_2 + parts_3
    groups = [(0, array, [part]) for array, part in zip(mine, own_parts)]
    groups += [
        (1, other_0, [(0, 0, 0, full)]),
        (1, other_1, parts_1),
        (1, other_2, parts_2),
        (1, other_3, parts_3),
    ]
    return label_blocks(groups)


def add_products(pieces, share, split, places, normed, cot, blocks, total, fresh):
    for number, (which, row, sub, rows) in enumerate(pieces):
        columns = pl.ds(pl.multiple_of(places[number] * share + sub, 128), rows)
        first = jnp.dot(
            normed[:, columns],
            blocks[which][row : row + rows, :split],
            preferred_element_type=jnp.float32,
        )
        second = jnp.dot(
            cot[:, columns],
            blocks[which][row : row + rows, split:],
            preferred_element_type=jnp.float32,
        )
        if fresh and number == 0:
            total[:, :split] = first
            total[:, split:] = second
        else:
            total[:, :split] += first
            total[:, split:] += second


def first_kernel(pieces, share, split, places, normed, cot, *refs):
    add_products(pieces, share, split, places, normed, cot, refs[:-1], refs[-1], True)


def project_kernel(pieces, share, split, places, normed, cot, begun, routing, flags, *refs):
    blocks, (out, total) = (refs[:-2], refs[-2:])
    total[...] = begun[...]
    add_products(pieces, share, split, places, normed, cot, blocks, total, False)
    width = total.shape[1]
    out[:, :width] = jnp.dot(
        routing[...], total[...].astype(jnp.bfloat16), preferred_element_type=jnp.float32
    ).astype(jnp.bfloat16)
    out[:, width:] = jnp.dot(
        routing[...], flags[...], preferred_element_type=jnp.float32
    ).astype(jnp.bfloat16)


def finish_kernel(pieces, share, split, places, both, tokens, cot, *refs):
    blocks, (result, grad, back) = (refs[:-3], refs[-3:])
    grad_rows = both[:, :split]
    attended = both[:, split:]
    rows_cols = (((1,), (1,)), ((), ()))
    for number, (which, row, sub, rows) in enumerate(pieces):
        columns = pl.ds(pl.multiple_of(places[number] * share + sub, 128), rows)
        back[:, columns] = lax.dot_general(
            grad_rows,
            blocks[which][row : row + rows, :split],
            rows_cols,
            preferred_element_type=jnp.float32,
        )
        added = lax.dot_general(
            attended,
            blocks[which][row : row + rows, split:],
            rows_cols,
            preferred_element_type=jnp.float32,
        )
        result[:, columns] = (tokens[:, columns].astype(jnp.float32) + added).astype(jnp.bfloat16)
    width = tokens.shape[1]
    values = tokens[...].astype(jnp.float32)
    squares = jnp.sum(values * values, axis=-1, keepdims=True)
    inverse = lax.rsqrt(squares / width + 1e-05)
    normed = values * inverse
    correction = jnp.sum(back[...] * normed, axis=-1, keepdims=True) / width
    grad[...] = (
        cot[...].astype(jnp.float32) + inverse * (back[...] - normed * correction)
    ).astype(jnp.bfloat16)


def weight_grad_kernel(row_pieces, col_pieces, split, *refs):
    inputs, (out, rows_all, cols_all) = (refs[:-3], refs[-3:])
    col_count = 1 + max(which for which, _, _ in col_pieces)
    share = cols_all.shape[1] // 2
    count = inputs[0].shape[2]
    for which, index, to in col_pieces:
        cols_all[to : to + count, :] = inputs[which][index]
    for which, row, to, rows in row_pieces:
        rows_all[to : to + rows, :] = inputs[col_count + which][row : row + rows, :]
    first = contract_rows(cols_all[:, :share], rows_all[:, :split]).astype(jnp.bfloat16)
    second = contract_rows(cols_all[:, share:], rows_all[:, split:]).astype(jnp.bfloat16)
    step = 128
    width = rows_all.shape[1]
    for at in range(0, width, step):
        piece = first[:, at : at + step] if at < split else second[:, at - split : at - split + step]
        out[at // step * share : at // step * share + share, :] = piece
    filled = width // step * share
    if filled < out.shape[0]:
        out[filled:, :] = jnp.zeros((out.shape[0] - filled, step), jnp.bfloat16)


def call(kernel, places, operands, out_shape, scratch, flops, read):
    vmem = pl.BlockSpec(memory_space=pltpu.VMEM)
    smem = [] if places is None else [pl.BlockSpec(memory_space=pltpu.SMEM)]
    return pl.pallas_call(
        kernel,
        out_shape=out_shape,
        in_specs=smem + [vmem] * len(operands),
        out_specs=jax.tree.map(lambda _: vmem, out_shape),
        scratch_shapes=scratch,
        cost_estimate=pl.CostEstimate(flops=flops, bytes_accessed=read, transcendentals=0),
    )(*([] if places is None else [places]), *operands)


def on_device(tokens, grad_out, qkv_weight, out_weight, range_len, doc_start):
    token_rows = tokens[0, 0]
    cot_rows = grad_out[0, 0]
    flag_rows = doc_start[0, 0].astype(jnp.bfloat16)
    lengths = range_len[0]
    row_count = token_rows.shape[0]
    model_width = token_rows.shape[1]
    qkv_width = qkv_weight.shape[1]
    out_width = out_weight.shape[1]
    groups = lax.axis_size(DP)
    owners = lax.axis_size(FSDP)
    my_index = lax.axis_index(DP)
    slot_count = 3 * row_count // 2 // groups
    total_slots = groups * slot_count
    range_end = jnp.cumsum(lengths, dtype=jnp.int32)
    starts = range_end - lengths
    pack_row = my_index + groups * jnp.arange(row_count, dtype=jnp.int32)
    target = jnp.sum(
        (range_end[None, :] <= pack_row[:, None]).astype(jnp.int32), axis=1, dtype=jnp.int32
    )
    range_ids = jnp.arange(groups, dtype=jnp.int32)
    range_first = jnp.sum(
        jnp.where(range_ids[None, :] == target[:, None], starts[None, :], 0),
        axis=1,
        dtype=jnp.int32,
    )
    flat_slot = target * slot_count + (pack_row - range_first) // groups
    routing = (jnp.arange(total_slots, dtype=jnp.int32)[:, None] == flat_slot[None, :]).astype(
        jnp.bfloat16
    )

    def from_slots(array):
        return contract_rows(routing, array.reshape(total_slots, -1)).astype(jnp.bfloat16)

    width = qkv_width + out_width
    share = model_width // owners
    order = [(dx, dy, dc) for dc in range(2) for dy in range(2) for dx in range(4)]
    piece = jax.ShapeDtypeStruct((2, 4, row_count, 2 * share), jnp.bfloat16)
    normed_b, keep, send = call(
        prepare_kernel,
        place_all(order),
        [token_rows, cot_rows],
        [jax.ShapeDtypeStruct((row_count, model_width), jnp.bfloat16), piece, piece],
        [],
        4 * row_count * model_width,
        10 * row_count * model_width,
    )
    flag_cols = jnp.broadcast_to(flag_rows[:, None], (row_count, 128))
    my_start = starts[my_index]
    my_length = lengths[my_index]
    source_ids = jnp.arange(groups, dtype=jnp.int32)[:, None]
    slot_ids = jnp.arange(slot_count, dtype=jnp.int32)[None, :]
    position = ((source_ids - my_start) % groups + groups * slot_ids).reshape(total_slots)
    other = swap_core(send)
    ahead = jnp.concatenate([keep[1], other[1]], axis=0)

    def first_dot(beside, arrays, pieces, places):
        return call(
            functools.partial(first_kernel, pieces, share, qkv_width),
            places,
            [beside[0], cot_rows, *arrays],
            jax.ShapeDtypeStruct((row_count, width), jnp.float32),
            [],
            row_count * model_width * width,
            model_width * width,
        )

    early, late, begun, beside = gather_weights(
        jnp.concatenate([qkv_weight, out_weight], axis=1),
        first_dot,
        (normed_b, keep, other, ahead, flag_cols, routing, position),
    )
    normed_b, keep, other, ahead, flag_cols, routing, position = beside
    slots = call(
        functools.partial(project_kernel, late[1], share, qkv_width),
        late[2],
        [normed_b, cot_rows, begun, routing, flag_cols, *late[0]],
        jax.ShapeDtypeStruct((total_slots, width + 128), jnp.bfloat16),
        [pltpu.VMEM((row_count, width), jnp.float32)],
        row_count * model_width * width,
        model_width * width,
    )
    blocks = [*early[0], *late[0]]
    pieces = early[1] + [(len(early[0]) + which, *rest) for which, *rest in late[1]]
    places = jnp.concatenate([early[2], late[2]])
    slots, keep, other, ahead = lax.optimization_barrier((slots, keep, other, ahead))
    got = swap_dp(slots.reshape(groups, slot_count, width + 128))
    cols, col_pieces = spread_cols(keep, other, ahead)
    got = got.reshape(total_slots, width + 128)
    both = call(
        functools.partial(attention_kernel, QH),
        my_length[None],
        [position[:, None], position[None, :], got],
        jax.ShapeDtypeStruct((total_slots, width), jnp.bfloat16),
        [],
        18 * total_slots * total_slots * out_width,
        4 * total_slots * width,
    )
    back = swap_dp(both.reshape(groups, slot_count, width))
    back, cols = lax.optimization_barrier((back, cols))
    both_rows = from_slots(back)
    row_blocks, row_pieces, row_offsets = gather_rows(both_rows)
    at = {offset: number * row_count for number, offset in enumerate(order)}
    row_pieces = [
        (which, row, at[offset] + sub, rows)
        for (which, row, sub, rows), offset in zip(row_pieces, row_offsets)
    ]
    col_pieces = [(which, index, at[offset]) for which, index, offset in col_pieces]
    each = -(-share * width // (128 * 8 * groups)) * 8
    partial = call(
        functools.partial(weight_grad_kernel, row_pieces, col_pieces, qkv_width),
        None,
        [*cols, *row_blocks],
        jax.ShapeDtypeStruct((groups * each, 128), jnp.bfloat16),
        [
            pltpu.VMEM((owners * row_count, width), jnp.bfloat16),
            pltpu.VMEM((owners * row_count, 2 * share), jnp.bfloat16),
        ],
        2 * owners * row_count * width * share,
        2 * owners * row_count * (width + 2 * share),
    )
    partial, both_late = lax.optimization_barrier((partial, both_rows))
    summed = sum_over_dp(partial.reshape(groups, each, 128))
    result, tokens_grad = call(
        functools.partial(finish_kernel, pieces, share, qkv_width),
        places,
        [both_late, token_rows, cot_rows, *blocks],
        [jax.ShapeDtypeStruct((row_count, model_width), jnp.bfloat16)] * 2,
        [pltpu.VMEM((row_count, model_width), jnp.float32)],
        2 * row_count * model_width * width,
        2 * model_width * width,
    )

    qkv_grad, out_grad = call(
        functools.partial(spread_kernel, qkv_width),
        None,
        [summed],
        [
            jax.ShapeDtypeStruct((share, qkv_width), jnp.float32),
            jax.ShapeDtypeStruct((share, out_width), jnp.float32),
        ],
        [],
        share * width,
        6 * share * width,
    )
    return (result[None, None], tokens_grad[None, None], qkv_grad, out_grad)


def swap_dp(array):
    return lax.all_to_all(array, DP, split_axis=0, concat_axis=0, tiled=True)


def sum_over_dp(partial):
    got = swap_dp(partial)
    mine = jnp.sum(got.astype(jnp.float32), axis=0).astype(jnp.bfloat16)
    return swap_dp(jnp.broadcast_to(mine[None], partial.shape)).reshape(-1, partial.shape[2])


def solution(mesh):
    fine = Mesh(mesh.devices.reshape(FINE), DP + FSDP)
    return jax.shard_map(
        on_device,
        mesh=fine,
        in_specs=(
            P(FSDP, DP, None, None),
            P(FSDP, DP, None, None),
            P(FSDP, None),
            P(FSDP, None),
            P(FSDP, None),
            P(FSDP, DP, None),
        ),
        out_specs=(
            P(FSDP, DP, None, None),
            P(FSDP, DP, None, None),
            P(FSDP, None),
            P(FSDP, None),
        ),
        check_vma=False,
    )
```

```python
import functools

import jax
import jax.numpy as jnp
from jax import lax
from jax.experimental import pallas as pl
from jax.experimental.pallas import tpu as pltpu
from jax.sharding import Mesh
from jax.sharding import PartitionSpec as P


QH = 4
DP = ("z", "yh")
FINE = (12, 4, 2, 4, 2)
FSDP = ("yl", "x", "core")


def prepare_kernel(places, tokens, cot, normed, keep, send):
    width = tokens.shape[1]
    share = keep.shape[3] // 2
    values = tokens[...].astype(jnp.float32)
    squares = jnp.sum(values * values, axis=-1, keepdims=True)
    normed[...] = (values * lax.rsqrt(squares / width + 1e-05)).astype(jnp.bfloat16)
    number = 0
    for out in (keep, send):
        for dx in range(out.shape[0]):
            for dy in range(out.shape[1]):
                columns = pl.ds(pl.multiple_of(places[number] * share, 128), share)
                out[dx, dy, :, :share] = normed[:, columns]
                out[dx, dy, :, share:] = cot[:, columns]
                number += 1


def contract_rows(left, right):
    return lax.dot_general(
        left, right, (((0,), (0,)), ((), ())), preferred_element_type=jnp.float32
    )


def contract_cols(left, right):
    return lax.dot_general(
        left, right, (((1,), (1,)), ((), ())), preferred_element_type=jnp.float32
    )


def attention_kernel(heads, length, place_col, place_row, got, out):
    size = got.shape[1] // (2 * heads + 3)
    wide = heads * size
    keys = got[:, wide : wide + size]
    values = got[:, wide + size : wide + 2 * size]
    flags = got[:, 2 * wide + 2 * size :].astype(jnp.float32)
    at_col, at_row = (place_col[...], place_row[...])
    live_col, live_row = (at_col < length[0], at_row < length[0])
    begin_col = (flags[:, :1] > 0) & live_col & (at_col > 0)
    begin_row = (flags.T[:1, :] > 0) & live_row & (at_row > 0)
    before = at_row <= at_col
    after = at_col <= at_row
    count_col = jnp.sum(jnp.where(before & begin_row, 1.0, 0.0), axis=1, keepdims=True)
    count_row = jnp.sum(jnp.where(after & begin_col, 1.0, 0.0), axis=0, keepdims=True)
    allowed = (before & (count_col == count_row) & live_col & live_row) | (at_row == at_col)
    scale = size ** (-0.5)
    grad_keys, grad_values = (0.0, 0.0)
    for head in range(heads):
        columns = slice(head * size, (head + 1) * size)
        queries = got[:, columns]
        grads = got[:, wide + 2 * size + head * size : wide + 2 * size + (head + 1) * size]
        scores = jnp.where(allowed, contract_cols(queries, keys) * scale, -1e30)
        exponent = jnp.exp(scores - jnp.max(scores, axis=-1, keepdims=True))
        weights = exponent / jnp.sum(exponent, axis=-1, keepdims=True)
        weights_b = weights.astype(jnp.bfloat16)
        attended = jnp.dot(weights_b, values, preferred_element_type=jnp.float32)
        attended = attended.astype(jnp.bfloat16)
        delta = jnp.sum(
            grads.astype(jnp.float32) * attended.astype(jnp.float32), axis=-1, keepdims=True
        )
        grad_scores = weights * (contract_cols(grads, values) - delta) * scale
        grad_scores = grad_scores.astype(jnp.bfloat16)
        out[:, columns] = jnp.dot(
            grad_scores, keys, preferred_element_type=jnp.float32
        ).astype(jnp.bfloat16)
        grad_keys += contract_rows(grad_scores, queries)
        grad_values += contract_rows(weights_b, grads)
        shifted = slice(wide + 2 * size + head * size, wide + 2 * size + (head + 1) * size)
        out[:, shifted] = attended
    out[:, wide : wide + size] = grad_keys.astype(jnp.bfloat16)
    out[:, wide + size : wide + 2 * size] = grad_values.astype(jnp.bfloat16)


def spread_kernel(split, whole, first, second):
    share = first.shape[0]
    for at in range(0, first.shape[1] + second.shape[1], 128):
        piece = whole[at // 128 * share : at // 128 * share + share, :].astype(jnp.float32)
        if at < split:
            first[:, at : at + 128] = piece
        else:
            second[:, at - split : at - split + 128] = piece


def shift_x(array, step):
    size = lax.axis_size("x")
    return lax.ppermute(array, "x", [(i, (i + step) % size) for i in range(size)])


def along_x(array):
    size = lax.axis_size("x")
    pairs = []
    for i in range(size):
        pairs.append((2 * i, (i + 1) % size * 2))
        pairs.append((2 * i + 1, (i - 1) % size * 2 + 1))
    return lax.ppermute(array, ("x", "core"), pairs)


def along_y(array):
    size = lax.axis_size(("yh", "yl"))
    pairs = []
    for i in range(size):
        pairs.append((2 * i, (i + 1) % size * 2))
        pairs.append((2 * i + 1, (i - 1) % size * 2 + 1))
    return lax.ppermute(array, ("yh", "yl", "core"), pairs)


def swap_y(array):
    return lax.ppermute(array, "yl", [(0, 1), (1, 0)])


def swap_core(array):
    return lax.ppermute(array, "core", [(0, 1), (1, 0)])


def place(dx, dy, dc):
    yl = (lax.axis_index("yl") + dy) % 2
    x = (lax.axis_index("x") + dx) % lax.axis_size("x")
    core = (lax.axis_index("core") + dc) % 2
    return ((yl * lax.axis_size("x") + x) * 2 + core).astype(jnp.int32)


def place_all(offsets):
    return jnp.stack([place(*offset) for offset in offsets])


def pack_x_kernel(keep, other, up, down):
    up[0] = keep[1]
    up[1] = other[1]
    up[2] = keep[2]
    down[0] = keep[3]
    down[1] = other[3]
    down[2] = other[2]


def pack_y_kernel(keep, other, up, down, far_up, far_down, out):
    out[0] = keep[0, 1]
    out[1] = other[0, 1]
    out[2] = up[0, 1]
    out[3] = up[1, 1]
    out[4] = down[0, 1]
    out[5] = down[1, 1]
    out[6] = far_up[1]
    out[7] = far_down[1]


def spread_cols(keep, other, up, down):
    piece = keep.shape[2:]
    up = shift_x(up, 1)
    down = shift_x(down, -1)
    far_up = shift_x(up[2], 1)
    far_down = shift_x(down[2], -1)
    arrays = [keep, other, up, down, far_up, far_down]
    packed = call(
        pack_y_kernel,
        None,
        arrays,
        jax.ShapeDtypeStruct((8, *piece), jnp.bfloat16),
        [],
        keep.size,
        4 * keep.size,
    )
    across = swap_y(packed)
    here = [(0, (0,), 0, 0), (1, (0,), 0, 1), (2, (0,), 3, 0), (2, (1,), 3, 1)]
    here += [(3, (0,), 1, 0), (3, (1,), 1, 1), (4, (), 2, 0), (5, (), 2, 1)]
    pieces = [(which, (*index, 0), (dx, 0, dc)) for which, index, dx, dc in here]
    pieces += [(6, (at,), (dx, 1, dc)) for at, (_, _, dx, dc) in enumerate(here)]
    return (arrays + [across], pieces)


def gather_weights(block, first_dot, beside):
    sign = 1 - 2 * lax.axis_index("core")
    near = along_x(block)
    across = along_y(block)
    other_0 = swap_core(block)
    next_block = along_x(other_0)
    side_a = along_y(near)
    far = along_x(near)
    next_block, beside = lax.optimization_barrier((next_block, beside))
    side_b = along_y(next_block)
    far_y = along_x(side_a)
    other_1 = swap_core(jnp.concatenate([near, next_block, across], axis=0))
    groups = [
        (block, [(0, 0, 0)]),
        (other_0, [(0, 0, 1)]),
        (near, [(-sign, 0, 0)]),
        (next_block, [(-sign, 0, 1)]),
        (across, [(0, 1, 0)]),
        (other_1, [(sign, 0, 1), (sign, 0, 0), (0, 1, 1)]),
    ]
    early = number_blocks(groups, place)
    total = first_dot(beside, *early)
    other_2 = swap_core(jnp.concatenate([side_a, side_b, far], axis=0))
    far_y, total = lax.optimization_barrier((far_y, total))
    other_3 = swap_core(far_y)
    groups = [
        (side_a, [(-sign, 1, 0)]),
        (side_b, [(-sign, 1, 1)]),
        (far, [(2, 0, 0)]),
        (far_y, [(2, 1, 0)]),
        (other_2, [(sign, 1, 1), (sign, 1, 0), (2, 0, 1)]),
        (other_3, [(2, 1, 1)]),
    ]
    return (early, number_blocks(groups, place), total, beside)


def row_slot(dx, dy, dc):
    return jnp.asarray((dc * 2 + dy) * 4 + dx % 4, jnp.int32)


def gather_rows(block):
    sign = 1 - 2 * lax.axis_index("core")
    near = along_x(block)
    across = swap_y(block)
    other_0 = swap_core(block)
    next_block = along_x(other_0)
    side_a = along_x(across)
    far = along_x(near)
    side_b = swap_y(next_block)
    far_y = along_x(side_a)
    other_1 = swap_core(jnp.concatenate([near, next_block, across], axis=0))
    other_2 = swap_core(jnp.concatenate([side_a, side_b, far, far_y], axis=0))
    groups = [
        (block, [(0, 0, 0)]),
        (other_0, [(0, 0, 1)]),
        (near, [(-sign, 0, 0)]),
        (next_block, [(-sign, 0, 1)]),
        (across, [(0, 1, 0)]),
        (other_1, [(sign, 0, 1), (sign, 0, 0), (0, 1, 1)]),
        (side_a, [(-sign, 1, 0)]),
        (side_b, [(-sign, 1, 1)]),
        (far, [(2, 0, 0)]),
        (far_y, [(2, 1, 0)]),
        (other_2, [(sign, 1, 1), (sign, 1, 0), (2, 0, 1), (2, 1, 1)]),
    ]
    return number_blocks(groups, row_slot)


def number_blocks(groups, numbering):
    arrays, pieces, places = [], [], []
    rows = groups[0][0].shape[0]
    for array, offsets in groups:
        for number, offset in enumerate(offsets):
            pieces.append((len(arrays), number * rows, 0, rows))
            places.append(numbering(*offset))
        arrays.append(array)
    return (arrays, pieces, jnp.stack(places))


def add_products(pieces, share, split, places, normed, cot, blocks, total, fresh):
    for number, (which, row, sub, rows) in enumerate(pieces):
        columns = pl.ds(pl.multiple_of(places[number] * share + sub, 128), rows)
        first = jnp.dot(
            normed[:, columns],
            blocks[which][row : row + rows, :split],
            preferred_element_type=jnp.float32,
        )
        second = jnp.dot(
            cot[:, columns],
            blocks[which][row : row + rows, split:],
            preferred_element_type=jnp.float32,
        )
        if fresh and number == 0:
            total[:, :split] = first
            total[:, split:] = second
        else:
            total[:, :split] += first
            total[:, split:] += second


def first_kernel(pieces, share, split, places, normed, cot, *refs):
    add_products(pieces, share, split, places, normed, cot, refs[:-1], refs[-1], True)


def project_kernel(pieces, share, split, places, normed, cot, begun, routing, flags, *refs):
    blocks, (out, total) = (refs[:-2], refs[-2:])
    total[...] = begun[...]
    add_products(pieces, share, split, places, normed, cot, blocks, total, False)
    width = total.shape[1]
    out[:, :width] = jnp.dot(
        routing[...], total[...].astype(jnp.bfloat16), preferred_element_type=jnp.float32
    ).astype(jnp.bfloat16)
    out[:, width:] = jnp.dot(
        routing[...], flags[...], preferred_element_type=jnp.float32
    ).astype(jnp.bfloat16)


def finish_kernel(pieces, share, split, places, both, tokens, cot, *refs):
    blocks, (result, grad, back) = (refs[:-3], refs[-3:])
    grad_rows = both[:, :split]
    attended = both[:, split:]
    rows_cols = (((1,), (1,)), ((), ()))
    for number, (which, row, sub, rows) in enumerate(pieces):
        columns = pl.ds(pl.multiple_of(places[number] * share + sub, 128), rows)
        back[:, columns] = lax.dot_general(
            grad_rows,
            blocks[which][row : row + rows, :split],
            rows_cols,
            preferred_element_type=jnp.float32,
        )
        added = lax.dot_general(
            attended,
            blocks[which][row : row + rows, split:],
            rows_cols,
            preferred_element_type=jnp.float32,
        )
        result[:, columns] = (tokens[:, columns].astype(jnp.float32) + added).astype(jnp.bfloat16)
    width = tokens.shape[1]
    values = tokens[...].astype(jnp.float32)
    squares = jnp.sum(values * values, axis=-1, keepdims=True)
    inverse = lax.rsqrt(squares / width + 1e-05)
    normed = values * inverse
    correction = jnp.sum(back[...] * normed, axis=-1, keepdims=True) / width
    grad[...] = (
        cot[...].astype(jnp.float32) + inverse * (back[...] - normed * correction)
    ).astype(jnp.bfloat16)


def weight_grad_kernel(row_pieces, col_pieces, split, slots, *refs):
    inputs, (out, rows_all, cols_all) = (refs[:-3], refs[-3:])
    col_count = 1 + max(which for which, _, _ in col_pieces)
    share = cols_all.shape[1] // 2
    count = inputs[0].shape[2]
    for which, index, to in col_pieces:
        cols_all[to : to + count, :] = inputs[which][index]
    for number, (which, row, _, rows) in enumerate(row_pieces):
        where = pl.ds(pl.multiple_of(slots[number] * count, 128), rows)
        rows_all[where, :] = inputs[col_count + which][row : row + rows, :]
    first = contract_rows(cols_all[:, :share], rows_all[:, :split]).astype(jnp.bfloat16)
    second = contract_rows(cols_all[:, share:], rows_all[:, split:]).astype(jnp.bfloat16)
    step = 128
    width = rows_all.shape[1]
    for at in range(0, width, step):
        piece = first[:, at : at + step] if at < split else second[:, at - split : at - split + step]
        out[at // step * share : at // step * share + share, :] = piece
    filled = width // step * share
    if filled < out.shape[0]:
        out[filled:, :] = jnp.zeros((out.shape[0] - filled, step), jnp.bfloat16)


def call(kernel, places, operands, out_shape, scratch, flops, read):
    vmem = pl.BlockSpec(memory_space=pltpu.VMEM)
    smem = [] if places is None else [pl.BlockSpec(memory_space=pltpu.SMEM)]
    return pl.pallas_call(
        kernel,
        out_shape=out_shape,
        in_specs=smem + [vmem] * len(operands),
        out_specs=jax.tree.map(lambda _: vmem, out_shape),
        scratch_shapes=scratch,
        cost_estimate=pl.CostEstimate(flops=flops, bytes_accessed=read, transcendentals=0),
    )(*([] if places is None else [places]), *operands)


def on_device(tokens, grad_out, qkv_weight, out_weight, range_len, doc_start):
    token_rows = tokens[0, 0]
    cot_rows = grad_out[0, 0]
    flag_rows = doc_start[0, 0].astype(jnp.bfloat16)
    lengths = range_len[0]
    row_count = token_rows.shape[0]
    model_width = token_rows.shape[1]
    qkv_width = qkv_weight.shape[1]
    out_width = out_weight.shape[1]
    groups = lax.axis_size(DP)
    owners = lax.axis_size(FSDP)
    my_index = lax.axis_index(DP)
    slot_count = 3 * row_count // 2 // groups
    total_slots = groups * slot_count
    range_end = jnp.cumsum(lengths, dtype=jnp.int32)
    starts = range_end - lengths
    pack_row = my_index + groups * jnp.arange(row_count, dtype=jnp.int32)
    target = jnp.sum(
        (range_end[None, :] <= pack_row[:, None]).astype(jnp.int32), axis=1, dtype=jnp.int32
    )
    range_ids = jnp.arange(groups, dtype=jnp.int32)
    range_first = jnp.sum(
        jnp.where(range_ids[None, :] == target[:, None], starts[None, :], 0),
        axis=1,
        dtype=jnp.int32,
    )
    flat_slot = target * slot_count + (pack_row - range_first) // groups
    routing = (jnp.arange(total_slots, dtype=jnp.int32)[:, None] == flat_slot[None, :]).astype(
        jnp.bfloat16
    )

    def from_slots(array):
        return contract_rows(routing, array.reshape(total_slots, -1)).astype(jnp.bfloat16)

    width = qkv_width + out_width
    share = model_width // owners
    order = [(dx, dy, dc) for dc in range(2) for dx in range(4) for dy in range(2)]
    piece = jax.ShapeDtypeStruct((4, 2, row_count, 2 * share), jnp.bfloat16)
    normed_b, keep, send = call(
        prepare_kernel,
        place_all(order),
        [token_rows, cot_rows],
        [jax.ShapeDtypeStruct((row_count, model_width), jnp.bfloat16), piece, piece],
        [],
        4 * row_count * model_width,
        10 * row_count * model_width,
    )
    flag_cols = jnp.broadcast_to(flag_rows[:, None], (row_count, 128))
    my_start = starts[my_index]
    my_length = lengths[my_index]
    source_ids = jnp.arange(groups, dtype=jnp.int32)[:, None]
    slot_ids = jnp.arange(slot_count, dtype=jnp.int32)[None, :]
    position = ((source_ids - my_start) % groups + groups * slot_ids).reshape(total_slots)
    other = swap_core(send)
    up, down = call(
        pack_x_kernel,
        None,
        [keep, other],
        [jax.ShapeDtypeStruct((3, *piece.shape[1:]), jnp.bfloat16)] * 2,
        [],
        keep.size,
        6 * keep.size,
    )

    def first_dot(beside, arrays, pieces, places):
        return call(
            functools.partial(first_kernel, pieces, share, qkv_width),
            places,
            [beside[0], cot_rows, *arrays],
            jax.ShapeDtypeStruct((row_count, width), jnp.float32),
            [],
            row_count * model_width * width,
            model_width * width,
        )

    early, late, begun, beside = gather_weights(
        jnp.concatenate([qkv_weight, out_weight], axis=1),
        first_dot,
        (normed_b, keep, other, up, down, flag_cols, routing, position),
    )
    normed_b, keep, other, up, down, flag_cols, routing, position = beside
    slots = call(
        functools.partial(project_kernel, late[1], share, qkv_width),
        late[2],
        [normed_b, cot_rows, begun, routing, flag_cols, *late[0]],
        jax.ShapeDtypeStruct((total_slots, width + 128), jnp.bfloat16),
        [pltpu.VMEM((row_count, width), jnp.float32)],
        row_count * model_width * width,
        model_width * width,
    )
    blocks = [*early[0], *late[0]]
    pieces = early[1] + [(len(early[0]) + which, *rest) for which, *rest in late[1]]
    places = jnp.concatenate([early[2], late[2]])
    slots, keep, other, up, down = lax.optimization_barrier((slots, keep, other, up, down))
    got = swap_dp(slots.reshape(groups, slot_count, width + 128))
    cols, col_pieces = spread_cols(keep, other, up, down)
    got = got.reshape(total_slots, width + 128)
    both = call(
        functools.partial(attention_kernel, QH),
        my_length[None],
        [position[:, None], position[None, :], got],
        jax.ShapeDtypeStruct((total_slots, width), jnp.bfloat16),
        [],
        18 * total_slots * total_slots * out_width,
        4 * total_slots * width,
    )
    back = swap_dp(both.reshape(groups, slot_count, width))
    back, cols = lax.optimization_barrier((back, cols))
    both_rows = from_slots(back)
    row_blocks, row_pieces, row_slots = gather_rows(both_rows)
    col_pieces = [
        (which, index, ((dc * 2 + dy) * 4 + dx) * row_count)
        for which, index, (dx, dy, dc) in col_pieces
    ]
    each = -(-share * width // (128 * 8 * groups)) * 8
    partial = call(
        functools.partial(weight_grad_kernel, row_pieces, col_pieces, qkv_width),
        row_slots,
        [*cols, *row_blocks],
        jax.ShapeDtypeStruct((groups * each, 128), jnp.bfloat16),
        [
            pltpu.VMEM((owners * row_count, width), jnp.bfloat16),
            pltpu.VMEM((owners * row_count, 2 * share), jnp.bfloat16),
        ],
        2 * owners * row_count * width * share,
        2 * owners * row_count * (width + 2 * share),
    )
    partial, both_late = lax.optimization_barrier((partial, both_rows))
    summed = sum_over_dp(partial.reshape(groups, each, 128))
    result, tokens_grad = call(
        functools.partial(finish_kernel, pieces, share, qkv_width),
        places,
        [both_late, token_rows, cot_rows, *blocks],
        [jax.ShapeDtypeStruct((row_count, model_width), jnp.bfloat16)] * 2,
        [pltpu.VMEM((row_count, model_width), jnp.float32)],
        2 * row_count * model_width * width,
        2 * model_width * width,
    )

    qkv_grad, out_grad = call(
        functools.partial(spread_kernel, qkv_width),
        None,
        [summed],
        [
            jax.ShapeDtypeStruct((share, qkv_width), jnp.float32),
            jax.ShapeDtypeStruct((share, out_width), jnp.float32),
        ],
        [],
        share * width,
        6 * share * width,
    )
    return (result[None, None], tokens_grad[None, None], qkv_grad, out_grad)


def swap_dp(array):
    return lax.all_to_all(array, DP, split_axis=0, concat_axis=0, tiled=True)


def sum_over_dp(partial):
    got = swap_dp(partial)
    mine = jnp.sum(got.astype(jnp.float32), axis=0).astype(jnp.bfloat16)
    return swap_dp(jnp.broadcast_to(mine[None], partial.shape)).reshape(-1, partial.shape[2])


def solution(mesh):
    fine = Mesh(mesh.devices.reshape(FINE), DP + FSDP)
    return jax.shard_map(
        on_device,
        mesh=fine,
        in_specs=(
            P(FSDP, DP, None, None),
            P(FSDP, DP, None, None),
            P(FSDP, None),
            P(FSDP, None),
            P(FSDP, None),
            P(FSDP, DP, None),
        ),
        out_specs=(
            P(FSDP, DP, None, None),
            P(FSDP, DP, None, None),
            P(FSDP, None),
            P(FSDP, None),
        ),
        check_vma=False,
    )
```

```python
import functools

import jax
import jax.numpy as jnp
from jax import lax
from jax.experimental import pallas as pl
from jax.experimental.pallas import tpu as pltpu
from jax.sharding import Mesh
from jax.sharding import PartitionSpec as P


QH = 4
DP = ("z", "yh")
FINE = (12, 4, 2, 4, 2)
FSDP = ("yl", "x", "core")


def prepare_kernel(places, tokens, cot, normed, keep, send):
    width = tokens.shape[1]
    share = keep.shape[3] // 2
    values = tokens[...].astype(jnp.float32)
    squares = jnp.sum(values * values, axis=-1, keepdims=True)
    normed[...] = (values * lax.rsqrt(squares / width + 1e-05)).astype(jnp.bfloat16)
    number = 0
    for out in (keep, send):
        for dx in range(out.shape[0]):
            for dy in range(out.shape[1]):
                columns = pl.ds(pl.multiple_of(places[number] * share, 128), share)
                out[dx, dy, :, :share] = normed[:, columns]
                out[dx, dy, :, share:] = cot[:, columns]
                number += 1


def contract_rows(left, right):
    return lax.dot_general(
        left, right, (((0,), (0,)), ((), ())), preferred_element_type=jnp.float32
    )


def contract_cols(left, right):
    return lax.dot_general(
        left, right, (((1,), (1,)), ((), ())), preferred_element_type=jnp.float32
    )


def attention_kernel(heads, length, place_col, place_row, got, out):
    size = got.shape[1] // (2 * heads + 3)
    wide = heads * size
    keys = got[:, wide : wide + size]
    values = got[:, wide + size : wide + 2 * size]
    flags = got[:, 2 * wide + 2 * size :].astype(jnp.float32)
    at_col, at_row = (place_col[...], place_row[...])
    live_col, live_row = (at_col < length[0], at_row < length[0])
    begin_col = (flags[:, :1] > 0) & live_col & (at_col > 0)
    begin_row = (flags.T[:1, :] > 0) & live_row & (at_row > 0)
    before = at_row <= at_col
    after = at_col <= at_row
    count_col = jnp.sum(jnp.where(before & begin_row, 1.0, 0.0), axis=1, keepdims=True)
    count_row = jnp.sum(jnp.where(after & begin_col, 1.0, 0.0), axis=0, keepdims=True)
    allowed = (before & (count_col == count_row) & live_col & live_row) | (at_row == at_col)
    scale = size ** (-0.5)
    grad_keys, grad_values = (0.0, 0.0)
    for head in range(heads):
        columns = slice(head * size, (head + 1) * size)
        queries = got[:, columns]
        grads = got[:, wide + 2 * size + head * size : wide + 2 * size + (head + 1) * size]
        scores = jnp.where(allowed, contract_cols(queries, keys) * scale, -1e30)
        exponent = jnp.exp(scores - jnp.max(scores, axis=-1, keepdims=True))
        weights = exponent / jnp.sum(exponent, axis=-1, keepdims=True)
        weights_b = weights.astype(jnp.bfloat16)
        attended = jnp.dot(weights_b, values, preferred_element_type=jnp.float32)
        attended = attended.astype(jnp.bfloat16)
        delta = jnp.sum(
            grads.astype(jnp.float32) * attended.astype(jnp.float32), axis=-1, keepdims=True
        )
        grad_scores = weights * (contract_cols(grads, values) - delta) * scale
        grad_scores = grad_scores.astype(jnp.bfloat16)
        out[:, columns] = jnp.dot(
            grad_scores, keys, preferred_element_type=jnp.float32
        ).astype(jnp.bfloat16)
        grad_keys += contract_rows(grad_scores, queries)
        grad_values += contract_rows(weights_b, grads)
        shifted = slice(wide + 2 * size + head * size, wide + 2 * size + (head + 1) * size)
        out[:, shifted] = attended
    out[:, wide : wide + size] = grad_keys.astype(jnp.bfloat16)
    out[:, wide + size : wide + 2 * size] = grad_values.astype(jnp.bfloat16)


def spread_kernel(split, whole, first, second):
    share = first.shape[0]
    for at in range(0, first.shape[1] + second.shape[1], 128):
        piece = whole[at // 128 * share : at // 128 * share + share, :].astype(jnp.float32)
        if at < split:
            first[:, at : at + 128] = piece
        else:
            second[:, at - split : at - split + 128] = piece


def shift_x(array, step):
    size = lax.axis_size("x")
    return lax.ppermute(array, "x", [(i, (i + step) % size) for i in range(size)])


def along_x(array):
    size = lax.axis_size("x")
    pairs = []
    for i in range(size):
        pairs.append((2 * i, (i + 1) % size * 2))
        pairs.append((2 * i + 1, (i - 1) % size * 2 + 1))
    return lax.ppermute(array, ("x", "core"), pairs)


def along_y(array):
    size = lax.axis_size(("yh", "yl"))
    pairs = []
    for i in range(size):
        pairs.append((2 * i, (i + 1) % size * 2))
        pairs.append((2 * i + 1, (i - 1) % size * 2 + 1))
    return lax.ppermute(array, ("yh", "yl", "core"), pairs)


def swap_y(array):
    return lax.ppermute(array, "yl", [(0, 1), (1, 0)])


def swap_core(array):
    return lax.ppermute(array, "core", [(0, 1), (1, 0)])


def place(dx, dy, dc):
    yl = (lax.axis_index("yl") + dy) % 2
    x = (lax.axis_index("x") + dx) % lax.axis_size("x")
    core = (lax.axis_index("core") + dc) % 2
    return ((yl * lax.axis_size("x") + x) * 2 + core).astype(jnp.int32)


def place_all(offsets):
    return jnp.stack([place(*offset) for offset in offsets])


def join_kernel(first, second, out):
    out[:, : first.shape[1]] = first[...]
    out[:, first.shape[1] :] = second[...]


def pack_x_kernel(keep, other, up, down):
    up[0] = keep[1]
    up[1] = other[1]
    up[2] = keep[2]
    down[0] = keep[3]
    down[1] = other[3]
    down[2] = other[2]


def pack_y_kernel(keep, other, up, down, far_up, far_down, out):
    out[0] = keep[0, 1]
    out[1] = other[0, 1]
    out[2] = up[0, 1]
    out[3] = up[1, 1]
    out[4] = down[0, 1]
    out[5] = down[1, 1]
    out[6] = far_up[1]
    out[7] = far_down[1]


def spread_cols(keep, other, up, down):
    piece = keep.shape[2:]
    up = shift_x(up, 1)
    down = shift_x(down, -1)
    far_up = shift_x(up[2], 1)
    far_down = shift_x(down[2], -1)
    arrays = [keep, other, up, down, far_up, far_down]
    packed = call(
        pack_y_kernel,
        None,
        arrays,
        jax.ShapeDtypeStruct((8, *piece), jnp.bfloat16),
        [],
        keep.size,
        4 * keep.size,
    )
    across = swap_y(packed)
    here = [(0, (0,), 0, 0), (1, (0,), 0, 1), (2, (0,), 3, 0), (2, (1,), 3, 1)]
    here += [(3, (0,), 1, 0), (3, (1,), 1, 1), (4, (), 2, 0), (5, (), 2, 1)]
    pieces = [(which, (*index, 0), (dx, 0, dc)) for which, index, dx, dc in here]
    pieces += [(6, (at,), (dx, 1, dc)) for at, (_, _, dx, dc) in enumerate(here)]
    return (arrays + [across], pieces)


def gather_weights(block, first_dot, beside):
    sign = 1 - 2 * lax.axis_index("core")
    near = along_x(block)
    across = along_y(block)
    other_0 = swap_core(block)
    next_block = along_x(other_0)
    side_a = along_y(near)
    far = along_x(near)
    side_b = along_y(next_block)
    far_y = along_x(side_a)
    other_1 = swap_core(jnp.concatenate([near, next_block, across], axis=0))
    groups = [
        (block, [(0, 0, 0)]),
        (other_0, [(0, 0, 1)]),
        (near, [(-sign, 0, 0)]),
        (next_block, [(-sign, 0, 1)]),
        (across, [(0, 1, 0)]),
        (other_1, [(sign, 0, 1), (sign, 0, 0), (0, 1, 1)]),
    ]
    early = number_blocks(groups, place)
    side_b, beside = lax.optimization_barrier((side_b, beside))
    total = first_dot(beside, *early)
    other_2 = swap_core(jnp.concatenate([side_a, side_b, far], axis=0))
    other_3 = swap_core(far_y)
    groups = [
        (side_a, [(-sign, 1, 0)]),
        (side_b, [(-sign, 1, 1)]),
        (far, [(2, 0, 0)]),
        (far_y, [(2, 1, 0)]),
        (other_2, [(sign, 1, 1), (sign, 1, 0), (2, 0, 1)]),
        (other_3, [(2, 1, 1)]),
    ]
    return (early, number_blocks(groups, place), total, beside)


def row_slot(dx, dy, dc):
    return jnp.asarray((dc * 2 + dy) * 4 + dx % 4, jnp.int32)


def gather_rows(block):
    sign = 1 - 2 * lax.axis_index("core")
    near = along_x(block)
    across = swap_y(block)
    other_0 = swap_core(block)
    next_block = along_x(other_0)
    side_a = along_x(across)
    far = along_x(near)
    side_b = swap_y(next_block)
    far_y = along_x(side_a)
    other_1 = swap_core(jnp.concatenate([near, next_block, across], axis=0))
    other_2 = swap_core(jnp.concatenate([side_a, side_b, far, far_y], axis=0))
    groups = [
        (block, [(0, 0, 0)]),
        (other_0, [(0, 0, 1)]),
        (near, [(-sign, 0, 0)]),
        (next_block, [(-sign, 0, 1)]),
        (across, [(0, 1, 0)]),
        (other_1, [(sign, 0, 1), (sign, 0, 0), (0, 1, 1)]),
        (side_a, [(-sign, 1, 0)]),
        (side_b, [(-sign, 1, 1)]),
        (far, [(2, 0, 0)]),
        (far_y, [(2, 1, 0)]),
        (other_2, [(sign, 1, 1), (sign, 1, 0), (2, 0, 1), (2, 1, 1)]),
    ]
    return number_blocks(groups, row_slot)


def number_blocks(groups, numbering):
    arrays, pieces, places = [], [], []
    rows = groups[0][0].shape[0]
    for array, offsets in groups:
        for number, offset in enumerate(offsets):
            pieces.append((len(arrays), number * rows, 0, rows))
            places.append(numbering(*offset))
        arrays.append(array)
    return (arrays, pieces, jnp.stack(places))


def add_products(pieces, share, split, places, normed, cot, blocks, total, fresh):
    for number, (which, row, sub, rows) in enumerate(pieces):
        columns = pl.ds(pl.multiple_of(places[number] * share + sub, 128), rows)
        first = jnp.dot(
            normed[:, columns],
            blocks[which][row : row + rows, :split],
            preferred_element_type=jnp.float32,
        )
        second = jnp.dot(
            cot[:, columns],
            blocks[which][row : row + rows, split:],
            preferred_element_type=jnp.float32,
        )
        if fresh and number == 0:
            total[:, :split] = first
            total[:, split:] = second
        else:
            total[:, :split] += first
            total[:, split:] += second


def first_kernel(pieces, share, split, places, normed, cot, *refs):
    add_products(pieces, share, split, places, normed, cot, refs[:-1], refs[-1], True)


def project_kernel(pieces, share, split, places, normed, cot, begun, routing, flags, *refs):
    blocks, (out, total) = (refs[:-2], refs[-2:])
    total[...] = begun[...]
    add_products(pieces, share, split, places, normed, cot, blocks, total, False)
    width = total.shape[1]
    out[:, :width] = jnp.dot(
        routing[...], total[...].astype(jnp.bfloat16), preferred_element_type=jnp.float32
    ).astype(jnp.bfloat16)
    out[:, width:] = jnp.dot(
        routing[...], flags[...], preferred_element_type=jnp.float32
    ).astype(jnp.bfloat16)


def finish_kernel(pieces, share, split, places, both, tokens, cot, *refs):
    blocks, (result, grad, back) = (refs[:-3], refs[-3:])
    grad_rows = both[:, :split]
    attended = both[:, split:]
    rows_cols = (((1,), (1,)), ((), ()))
    for number, (which, row, sub, rows) in enumerate(pieces):
        columns = pl.ds(pl.multiple_of(places[number] * share + sub, 128), rows)
        back[:, columns] = lax.dot_general(
            grad_rows,
            blocks[which][row : row + rows, :split],
            rows_cols,
            preferred_element_type=jnp.float32,
        )
        added = lax.dot_general(
            attended,
            blocks[which][row : row + rows, split:],
            rows_cols,
            preferred_element_type=jnp.float32,
        )
        result[:, columns] = (tokens[:, columns].astype(jnp.float32) + added).astype(jnp.bfloat16)
    width = tokens.shape[1]
    values = tokens[...].astype(jnp.float32)
    squares = jnp.sum(values * values, axis=-1, keepdims=True)
    inverse = lax.rsqrt(squares / width + 1e-05)
    normed = values * inverse
    correction = jnp.sum(back[...] * normed, axis=-1, keepdims=True) / width
    grad[...] = (
        cot[...].astype(jnp.float32) + inverse * (back[...] - normed * correction)
    ).astype(jnp.bfloat16)


def weight_grad_kernel(row_pieces, col_pieces, split, slots, *refs):
    inputs, (out, rows_all, cols_all) = (refs[:-3], refs[-3:])
    col_count = 1 + max(which for which, _, _ in col_pieces)
    share = cols_all.shape[1] // 2
    count = inputs[0].shape[2]
    for which, index, to in col_pieces:
        cols_all[to : to + count, :] = inputs[which][index]
    for number, (which, row, _, rows) in enumerate(row_pieces):
        where = pl.ds(pl.multiple_of(slots[number] * count, 128), rows)
        rows_all[where, :] = inputs[col_count + which][row : row + rows, :]
    first = contract_rows(cols_all[:, :share], rows_all[:, :split]).astype(jnp.bfloat16)
    second = contract_rows(cols_all[:, share:], rows_all[:, split:]).astype(jnp.bfloat16)
    step = 128
    width = rows_all.shape[1]
    for at in range(0, width, step):
        piece = first[:, at : at + step] if at < split else second[:, at - split : at - split + step]
        out[at // step * share : at // step * share + share, :] = piece
    filled = width // step * share
    if filled < out.shape[0]:
        out[filled:, :] = jnp.zeros((out.shape[0] - filled, step), jnp.bfloat16)


def call(kernel, places, operands, out_shape, scratch, flops, read):
    vmem = pl.BlockSpec(memory_space=pltpu.VMEM)
    smem = [] if places is None else [pl.BlockSpec(memory_space=pltpu.SMEM)]
    return pl.pallas_call(
        kernel,
        out_shape=out_shape,
        in_specs=smem + [vmem] * len(operands),
        out_specs=jax.tree.map(lambda _: vmem, out_shape),
        scratch_shapes=scratch,
        cost_estimate=pl.CostEstimate(flops=flops, bytes_accessed=read, transcendentals=0),
    )(*([] if places is None else [places]), *operands)


def on_device(tokens, grad_out, qkv_weight, out_weight, range_len, doc_start):
    token_rows = tokens[0, 0]
    cot_rows = grad_out[0, 0]
    flag_rows = doc_start[0, 0].astype(jnp.bfloat16)
    lengths = range_len[0]
    row_count = token_rows.shape[0]
    model_width = token_rows.shape[1]
    qkv_width = qkv_weight.shape[1]
    out_width = out_weight.shape[1]
    groups = lax.axis_size(DP)
    owners = lax.axis_size(FSDP)
    my_index = lax.axis_index(DP)
    slot_count = 3 * row_count // 2 // groups
    total_slots = groups * slot_count
    range_end = jnp.cumsum(lengths, dtype=jnp.int32)
    starts = range_end - lengths
    pack_row = my_index + groups * jnp.arange(row_count, dtype=jnp.int32)
    target = jnp.sum(
        (range_end[None, :] <= pack_row[:, None]).astype(jnp.int32), axis=1, dtype=jnp.int32
    )
    range_ids = jnp.arange(groups, dtype=jnp.int32)
    range_first = jnp.sum(
        jnp.where(range_ids[None, :] == target[:, None], starts[None, :], 0),
        axis=1,
        dtype=jnp.int32,
    )
    flat_slot = target * slot_count + (pack_row - range_first) // groups
    routing = (jnp.arange(total_slots, dtype=jnp.int32)[:, None] == flat_slot[None, :]).astype(
        jnp.bfloat16
    )

    def from_slots(array):
        return contract_rows(routing, array.reshape(total_slots, -1)).astype(jnp.bfloat16)

    width = qkv_width + out_width
    share = model_width // owners
    order = [(dx, dy, dc) for dc in range(2) for dx in range(4) for dy in range(2)]
    piece = jax.ShapeDtypeStruct((4, 2, row_count, 2 * share), jnp.bfloat16)
    normed_b, keep, send = call(
        prepare_kernel,
        place_all(order),
        [token_rows, cot_rows],
        [jax.ShapeDtypeStruct((row_count, model_width), jnp.bfloat16), piece, piece],
        [],
        4 * row_count * model_width,
        10 * row_count * model_width,
    )
    flag_cols = jnp.broadcast_to(flag_rows[:, None], (row_count, 128))
    my_start = starts[my_index]
    my_length = lengths[my_index]
    source_ids = jnp.arange(groups, dtype=jnp.int32)[:, None]
    slot_ids = jnp.arange(slot_count, dtype=jnp.int32)[None, :]
    position = ((source_ids - my_start) % groups + groups * slot_ids).reshape(total_slots)
    other = swap_core(send)
    up, down = call(
        pack_x_kernel,
        None,
        [keep, other],
        [jax.ShapeDtypeStruct((3, *piece.shape[1:]), jnp.bfloat16)] * 2,
        [],
        keep.size,
        6 * keep.size,
    )

    def first_dot(beside, arrays, pieces, places):
        return call(
            functools.partial(first_kernel, pieces, share, qkv_width),
            places,
            [beside[0], cot_rows, *arrays],
            jax.ShapeDtypeStruct((row_count, width), jnp.float32),
            [],
            row_count * model_width * width,
            model_width * width,
        )

    early, late, begun, beside = gather_weights(
        call(
            join_kernel,
            None,
            [qkv_weight, out_weight],
            jax.ShapeDtypeStruct((share, width), jnp.bfloat16),
            [],
            share * width,
            4 * share * width,
        ),
        first_dot,
        (normed_b, keep, other, up, down, flag_cols, routing, position),
    )
    normed_b, keep, other, up, down, flag_cols, routing, position = beside
    slots = call(
        functools.partial(project_kernel, late[1], share, qkv_width),
        late[2],
        [normed_b, cot_rows, begun, routing, flag_cols, *late[0]],
        jax.ShapeDtypeStruct((total_slots, width + 128), jnp.bfloat16),
        [pltpu.VMEM((row_count, width), jnp.float32)],
        row_count * model_width * width,
        model_width * width,
    )
    blocks = [*early[0], *late[0]]
    pieces = early[1] + [(len(early[0]) + which, *rest) for which, *rest in late[1]]
    places = jnp.concatenate([early[2], late[2]])
    slots, keep, other, up, down = lax.optimization_barrier((slots, keep, other, up, down))
    got = swap_dp(slots.reshape(groups, slot_count, width + 128))
    cols, col_pieces = spread_cols(keep, other, up, down)
    got = got.reshape(total_slots, width + 128)
    both = call(
        functools.partial(attention_kernel, QH),
        my_length[None],
        [position[:, None], position[None, :], got],
        jax.ShapeDtypeStruct((total_slots, width), jnp.bfloat16),
        [],
        18 * total_slots * total_slots * out_width,
        4 * total_slots * width,
    )
    back = swap_dp(both.reshape(groups, slot_count, width))
    back, cols = lax.optimization_barrier((back, cols))
    both_rows = from_slots(back)
    row_blocks, row_pieces, row_slots = gather_rows(both_rows)
    col_pieces = [
        (which, index, ((dc * 2 + dy) * 4 + dx) * row_count)
        for which, index, (dx, dy, dc) in col_pieces
    ]
    each = -(-share * width // (128 * 8 * groups)) * 8
    partial = call(
        functools.partial(weight_grad_kernel, row_pieces, col_pieces, qkv_width),
        row_slots,
        [*cols, *row_blocks],
        jax.ShapeDtypeStruct((groups * each, 128), jnp.bfloat16),
        [
            pltpu.VMEM((owners * row_count, width), jnp.bfloat16),
            pltpu.VMEM((owners * row_count, 2 * share), jnp.bfloat16),
        ],
        2 * owners * row_count * width * share,
        2 * owners * row_count * (width + 2 * share),
    )
    partial, both_late = lax.optimization_barrier((partial, both_rows))
    summed = sum_over_dp(partial.reshape(groups, each, 128))
    result, tokens_grad = call(
        functools.partial(finish_kernel, pieces, share, qkv_width),
        places,
        [both_late, token_rows, cot_rows, *blocks],
        [jax.ShapeDtypeStruct((row_count, model_width), jnp.bfloat16)] * 2,
        [pltpu.VMEM((row_count, model_width), jnp.float32)],
        2 * row_count * model_width * width,
        2 * model_width * width,
    )

    qkv_grad, out_grad = call(
        functools.partial(spread_kernel, qkv_width),
        None,
        [summed],
        [
            jax.ShapeDtypeStruct((share, qkv_width), jnp.float32),
            jax.ShapeDtypeStruct((share, out_width), jnp.float32),
        ],
        [],
        share * width,
        6 * share * width,
    )
    return (result[None, None], tokens_grad[None, None], qkv_grad, out_grad)


def swap_dp(array):
    return lax.all_to_all(array, DP, split_axis=0, concat_axis=0, tiled=True)


def sum_over_dp(partial):
    got = swap_dp(partial)
    mine = jnp.sum(got.astype(jnp.float32), axis=0).astype(jnp.bfloat16)
    return swap_dp(jnp.broadcast_to(mine[None], partial.shape)).reshape(-1, partial.shape[2])


def solution(mesh):
    fine = Mesh(mesh.devices.reshape(FINE), DP + FSDP)
    return jax.shard_map(
        on_device,
        mesh=fine,
        in_specs=(
            P(FSDP, DP, None, None),
            P(FSDP, DP, None, None),
            P(FSDP, None),
            P(FSDP, None),
            P(FSDP, None),
            P(FSDP, DP, None),
        ),
        out_specs=(
            P(FSDP, DP, None, None),
            P(FSDP, DP, None, None),
            P(FSDP, None),
            P(FSDP, None),
        ),
        check_vma=False,
    )
```

```python
import functools

import jax
import jax.numpy as jnp
from jax import lax
from jax.experimental import pallas as pl
from jax.experimental.pallas import tpu as pltpu
from jax.sharding import Mesh
from jax.sharding import PartitionSpec as P


QH = 4
DP = ("z", "yh")
FINE = (12, 4, 2, 4, 2)
FSDP = ("yl", "x", "core")


def prepare_kernel(places, tokens, cot, normed, keep, send):
    width = tokens.shape[1]
    share = keep.shape[3] // 2
    values = tokens[...].astype(jnp.float32)
    squares = jnp.sum(values * values, axis=-1, keepdims=True)
    normed[...] = (values * lax.rsqrt(squares / width + 1e-05)).astype(jnp.bfloat16)
    number = 0
    for out in (keep, send):
        for dx in range(out.shape[0]):
            for dy in range(out.shape[1]):
                columns = pl.ds(pl.multiple_of(places[number] * share, 128), share)
                out[dx, dy, :, :share] = normed[:, columns]
                out[dx, dy, :, share:] = cot[:, columns]
                number += 1


def contract_rows(left, right):
    return lax.dot_general(
        left, right, (((0,), (0,)), ((), ())), preferred_element_type=jnp.float32
    )


def contract_cols(left, right):
    return lax.dot_general(
        left, right, (((1,), (1,)), ((), ())), preferred_element_type=jnp.float32
    )


def attention_kernel(heads, length, place_col, place_row, got, out):
    size = got.shape[1] // (2 * heads + 3)
    wide = heads * size
    keys = got[:, wide : wide + size]
    values = got[:, wide + size : wide + 2 * size]
    flags = got[:, 2 * wide + 2 * size :].astype(jnp.float32)
    at_col, at_row = (place_col[...], place_row[...])
    live_col, live_row = (at_col < length[0], at_row < length[0])
    begin_col = (flags[:, :1] > 0) & live_col & (at_col > 0)
    begin_row = (flags.T[:1, :] > 0) & live_row & (at_row > 0)
    before = at_row <= at_col
    after = at_col <= at_row
    count_col = jnp.sum(jnp.where(before & begin_row, 1.0, 0.0), axis=1, keepdims=True)
    count_row = jnp.sum(jnp.where(after & begin_col, 1.0, 0.0), axis=0, keepdims=True)
    allowed = (before & (count_col == count_row) & live_col & live_row) | (at_row == at_col)
    scale = size ** (-0.5)
    grad_keys, grad_values = (0.0, 0.0)
    for head in range(heads):
        columns = slice(head * size, (head + 1) * size)
        queries = got[:, columns]
        grads = got[:, wide + 2 * size + head * size : wide + 2 * size + (head + 1) * size]
        scores = jnp.where(allowed, contract_cols(queries, keys) * scale, -1e30)
        exponent = jnp.exp(scores - jnp.max(scores, axis=-1, keepdims=True))
        weights = exponent / jnp.sum(exponent, axis=-1, keepdims=True)
        weights_b = weights.astype(jnp.bfloat16)
        attended = jnp.dot(weights_b, values, preferred_element_type=jnp.float32)
        attended = attended.astype(jnp.bfloat16)
        delta = jnp.sum(
            grads.astype(jnp.float32) * attended.astype(jnp.float32), axis=-1, keepdims=True
        )
        grad_scores = weights * (contract_cols(grads, values) - delta) * scale
        grad_scores = grad_scores.astype(jnp.bfloat16)
        out[:, columns] = jnp.dot(
            grad_scores, keys, preferred_element_type=jnp.float32
        ).astype(jnp.bfloat16)
        grad_keys += contract_rows(grad_scores, queries)
        grad_values += contract_rows(weights_b, grads)
        shifted = slice(wide + 2 * size + head * size, wide + 2 * size + (head + 1) * size)
        out[:, shifted] = attended
    out[:, wide : wide + size] = grad_keys.astype(jnp.bfloat16)
    out[:, wide + size : wide + 2 * size] = grad_values.astype(jnp.bfloat16)


def spread_kernel(split, whole, first, second):
    share = first.shape[0]
    for at in range(0, first.shape[1] + second.shape[1], 128):
        piece = whole[at // 128 * share : at // 128 * share + share, :].astype(jnp.float32)
        if at < split:
            first[:, at : at + 128] = piece
        else:
            second[:, at - split : at - split + 128] = piece


def shift_x(array, step):
    size = lax.axis_size("x")
    return lax.ppermute(array, "x", [(i, (i + step) % size) for i in range(size)])


def along_x(array):
    size = lax.axis_size("x")
    pairs = []
    for i in range(size):
        pairs.append((2 * i, (i + 1) % size * 2))
        pairs.append((2 * i + 1, (i - 1) % size * 2 + 1))
    return lax.ppermute(array, ("x", "core"), pairs)


def along_y(array):
    size = lax.axis_size(("yh", "yl"))
    pairs = []
    for i in range(size):
        pairs.append((2 * i, (i + 1) % size * 2))
        pairs.append((2 * i + 1, (i - 1) % size * 2 + 1))
    return lax.ppermute(array, ("yh", "yl", "core"), pairs)


def swap_y(array):
    return lax.ppermute(array, "yl", [(0, 1), (1, 0)])


def swap_core(array):
    return lax.ppermute(array, "core", [(0, 1), (1, 0)])


def place(dx, dy, dc):
    yl = (lax.axis_index("yl") + dy) % 2
    x = (lax.axis_index("x") + dx) % lax.axis_size("x")
    core = (lax.axis_index("core") + dc) % 2
    return ((yl * lax.axis_size("x") + x) * 2 + core).astype(jnp.int32)


def place_all(offsets):
    return jnp.stack([place(*offset) for offset in offsets])


def join_kernel(first, second, out):
    out[:, : first.shape[1]] = first[...]
    out[:, first.shape[1] :] = second[...]


def pack_x_kernel(keep, other, up, down):
    up[0] = keep[1]
    up[1] = other[1]
    up[2] = keep[2]
    down[0] = keep[3]
    down[1] = other[3]
    down[2] = other[2]


def pack_y_kernel(keep, other, up, down, far_up, far_down, out):
    out[0] = keep[0, 1]
    out[1] = other[0, 1]
    out[2] = up[0, 1]
    out[3] = up[1, 1]
    out[4] = down[0, 1]
    out[5] = down[1, 1]
    out[6] = far_up[1]
    out[7] = far_down[1]


def spread_cols(keep, other, up, down):
    piece = keep.shape[2:]
    up = shift_x(up, 1)
    down = shift_x(down, -1)
    far_up = shift_x(up[2], 1)
    far_down = shift_x(down[2], -1)
    arrays = [keep, other, up, down, far_up, far_down]
    packed = call(
        pack_y_kernel,
        None,
        arrays,
        jax.ShapeDtypeStruct((8, *piece), jnp.bfloat16),
        [],
        keep.size,
        4 * keep.size,
    )
    across = swap_y(packed)
    here = [(0, (0,), 0, 0), (1, (0,), 0, 1), (2, (0,), 3, 0), (2, (1,), 3, 1)]
    here += [(3, (0,), 1, 0), (3, (1,), 1, 1), (4, (), 2, 0), (5, (), 2, 1)]
    pieces = [(which, (*index, 0), (dx, 0, dc)) for which, index, dx, dc in here]
    pieces += [(6, (at,), (dx, 1, dc)) for at, (_, _, dx, dc) in enumerate(here)]
    return (arrays + [across], pieces)


def gather_weights(block, first_dot, beside):
    sign = 1 - 2 * lax.axis_index("core")
    near = along_x(block)
    across = along_y(block)
    other_0 = swap_core(block)
    next_block = along_x(other_0)
    side_a = along_y(near)
    far = along_x(near)
    side_b = along_y(next_block)
    far_y = along_x(side_a)
    other_1 = swap_core(jnp.concatenate([near, next_block, across], axis=0))
    groups = [
        (block, [(0, 0, 0)]),
        (other_0, [(0, 0, 1)]),
        (near, [(-sign, 0, 0)]),
        (next_block, [(-sign, 0, 1)]),
        (across, [(0, 1, 0)]),
        (other_1, [(sign, 0, 1), (sign, 0, 0), (0, 1, 1)]),
    ]
    early = number_blocks(groups, place)
    side_b, beside = lax.optimization_barrier((side_b, beside))
    total = first_dot(beside, *early)
    other_2 = swap_core(jnp.concatenate([side_a, side_b, far], axis=0))
    other_3 = swap_core(far_y)
    groups = [
        (side_a, [(-sign, 1, 0)]),
        (side_b, [(-sign, 1, 1)]),
        (far, [(2, 0, 0)]),
        (far_y, [(2, 1, 0)]),
        (other_2, [(sign, 1, 1), (sign, 1, 0), (2, 0, 1)]),
        (other_3, [(2, 1, 1)]),
    ]
    return (early, number_blocks(groups, place), total, beside)


def row_slot(dx, dy, dc):
    return jnp.asarray((dc * 2 + dy) * 4 + dx % 4, jnp.int32)


def gather_rows(block):
    sign = 1 - 2 * lax.axis_index("core")
    near = along_x(block)
    across = swap_y(block)
    other_0 = swap_core(block)
    next_block = along_x(other_0)
    side_a = along_x(across)
    far = along_x(near)
    side_b = swap_y(next_block)
    far_y = along_x(side_a)
    other_1 = swap_core(jnp.concatenate([near, next_block, across], axis=0))
    other_2 = swap_core(jnp.concatenate([side_a, side_b, far, far_y], axis=0))
    groups = [
        (block, [(0, 0, 0)]),
        (other_0, [(0, 0, 1)]),
        (near, [(-sign, 0, 0)]),
        (next_block, [(-sign, 0, 1)]),
        (across, [(0, 1, 0)]),
        (other_1, [(sign, 0, 1), (sign, 0, 0), (0, 1, 1)]),
        (side_a, [(-sign, 1, 0)]),
        (side_b, [(-sign, 1, 1)]),
        (far, [(2, 0, 0)]),
        (far_y, [(2, 1, 0)]),
        (other_2, [(sign, 1, 1), (sign, 1, 0), (2, 0, 1), (2, 1, 1)]),
    ]
    return number_blocks(groups, row_slot)


def number_blocks(groups, numbering):
    arrays, pieces, places = [], [], []
    rows = groups[0][0].shape[0]
    for array, offsets in groups:
        for number, offset in enumerate(offsets):
            pieces.append((len(arrays), number * rows, 0, rows))
            places.append(numbering(*offset))
        arrays.append(array)
    return (arrays, pieces, jnp.stack(places))


def add_products(pieces, share, split, places, normed, cot, blocks, total, fresh):
    for number, (which, row, sub, rows) in enumerate(pieces):
        columns = pl.ds(pl.multiple_of(places[number] * share + sub, 128), rows)
        first = jnp.dot(
            normed[:, columns],
            blocks[which][row : row + rows, :split],
            preferred_element_type=jnp.float32,
        )
        second = jnp.dot(
            cot[:, columns],
            blocks[which][row : row + rows, split:],
            preferred_element_type=jnp.float32,
        )
        if fresh and number == 0:
            total[:, :split] = first
            total[:, split:] = second
        else:
            total[:, :split] += first
            total[:, split:] += second


def first_kernel(pieces, share, split, places, normed, cot, *refs):
    add_products(pieces, share, split, places, normed, cot, refs[:-1], refs[-1], True)


def project_kernel(pieces, share, split, places, normed, cot, begun, routing, flags, *refs):
    blocks, (out, total) = (refs[:-2], refs[-2:])
    total[...] = begun[...]
    add_products(pieces, share, split, places, normed, cot, blocks, total, False)
    width = total.shape[1]
    out[:, :width] = jnp.dot(
        routing[...], total[...].astype(jnp.bfloat16), preferred_element_type=jnp.float32
    ).astype(jnp.bfloat16)
    out[:, width:] = jnp.dot(
        routing[...], flags[...], preferred_element_type=jnp.float32
    ).astype(jnp.bfloat16)


def finish_kernel(pieces, share, split, places, both, tokens, cot, *refs):
    blocks, (result, grad, back) = (refs[:-3], refs[-3:])
    grad_rows = both[:, :split]
    attended = both[:, split:]
    rows_cols = (((1,), (1,)), ((), ()))
    for number, (which, row, sub, rows) in enumerate(pieces):
        columns = pl.ds(pl.multiple_of(places[number] * share + sub, 128), rows)
        back[:, columns] = lax.dot_general(
            grad_rows,
            blocks[which][row : row + rows, :split],
            rows_cols,
            preferred_element_type=jnp.float32,
        )
        added = lax.dot_general(
            attended,
            blocks[which][row : row + rows, split:],
            rows_cols,
            preferred_element_type=jnp.float32,
        )
        result[:, columns] = (tokens[:, columns].astype(jnp.float32) + added).astype(jnp.bfloat16)
    width = tokens.shape[1]
    values = tokens[...].astype(jnp.float32)
    squares = jnp.sum(values * values, axis=-1, keepdims=True)
    inverse = lax.rsqrt(squares / width + 1e-05)
    normed = values * inverse
    correction = jnp.sum(back[...] * normed, axis=-1, keepdims=True) / width
    grad[...] = (
        cot[...].astype(jnp.float32) + inverse * (back[...] - normed * correction)
    ).astype(jnp.bfloat16)


def turn_kernel(col_pieces, *refs):
    inputs, out = (refs[:-1], refs[-1])
    for which, index, to in col_pieces:
        piece = inputs[which][index]
        out[:, to : to + piece.shape[0]] = piece.T


def weight_grad_kernel(row_pieces, split, slots, turned, *refs):
    inputs, (out, rows_all) = (refs[:-2], refs[-2:])
    share = turned.shape[0] // 2
    for number, (which, row, _, rows) in enumerate(row_pieces):
        where = pl.ds(pl.multiple_of(slots[number] * rows, 128), rows)
        rows_all[where, :] = inputs[which][row : row + rows, :]
    first = jnp.dot(
        turned[:share, :], rows_all[:, :split], preferred_element_type=jnp.float32
    ).astype(jnp.bfloat16)
    second = jnp.dot(
        turned[share:, :], rows_all[:, split:], preferred_element_type=jnp.float32
    ).astype(jnp.bfloat16)
    step = 128
    width = rows_all.shape[1]
    for at in range(0, width, step):
        piece = first[:, at : at + step] if at < split else second[:, at - split : at - split + step]
        out[at // step * share : at // step * share + share, :] = piece
    filled = width // step * share
    if filled < out.shape[0]:
        out[filled:, :] = jnp.zeros((out.shape[0] - filled, step), jnp.bfloat16)


def call(kernel, places, operands, out_shape, scratch, flops, read):
    vmem = pl.BlockSpec(memory_space=pltpu.VMEM)
    smem = [] if places is None else [pl.BlockSpec(memory_space=pltpu.SMEM)]
    return pl.pallas_call(
        kernel,
        out_shape=out_shape,
        in_specs=smem + [vmem] * len(operands),
        out_specs=jax.tree.map(lambda _: vmem, out_shape),
        scratch_shapes=scratch,
        cost_estimate=pl.CostEstimate(flops=flops, bytes_accessed=read, transcendentals=0),
    )(*([] if places is None else [places]), *operands)


def on_device(tokens, grad_out, qkv_weight, out_weight, range_len, doc_start):
    token_rows = tokens[0, 0]
    cot_rows = grad_out[0, 0]
    flag_rows = doc_start[0, 0].astype(jnp.bfloat16)
    lengths = range_len[0]
    row_count = token_rows.shape[0]
    model_width = token_rows.shape[1]
    qkv_width = qkv_weight.shape[1]
    out_width = out_weight.shape[1]
    groups = lax.axis_size(DP)
    owners = lax.axis_size(FSDP)
    my_index = lax.axis_index(DP)
    slot_count = 3 * row_count // 2 // groups
    total_slots = groups * slot_count
    range_end = jnp.cumsum(lengths, dtype=jnp.int32)
    starts = range_end - lengths
    pack_row = my_index + groups * jnp.arange(row_count, dtype=jnp.int32)
    target = jnp.sum(
        (range_end[None, :] <= pack_row[:, None]).astype(jnp.int32), axis=1, dtype=jnp.int32
    )
    range_ids = jnp.arange(groups, dtype=jnp.int32)
    range_first = jnp.sum(
        jnp.where(range_ids[None, :] == target[:, None], starts[None, :], 0),
        axis=1,
        dtype=jnp.int32,
    )
    flat_slot = target * slot_count + (pack_row - range_first) // groups
    routing = (jnp.arange(total_slots, dtype=jnp.int32)[:, None] == flat_slot[None, :]).astype(
        jnp.bfloat16
    )

    def from_slots(array):
        return contract_rows(routing, array.reshape(total_slots, -1)).astype(jnp.bfloat16)

    width = qkv_width + out_width
    share = model_width // owners
    order = [(dx, dy, dc) for dc in range(2) for dx in range(4) for dy in range(2)]
    piece = jax.ShapeDtypeStruct((4, 2, row_count, 2 * share), jnp.bfloat16)
    normed_b, keep, send = call(
        prepare_kernel,
        place_all(order),
        [token_rows, cot_rows],
        [jax.ShapeDtypeStruct((row_count, model_width), jnp.bfloat16), piece, piece],
        [],
        4 * row_count * model_width,
        10 * row_count * model_width,
    )
    flag_cols = jnp.broadcast_to(flag_rows[:, None], (row_count, 128))
    my_start = starts[my_index]
    my_length = lengths[my_index]
    source_ids = jnp.arange(groups, dtype=jnp.int32)[:, None]
    slot_ids = jnp.arange(slot_count, dtype=jnp.int32)[None, :]
    position = ((source_ids - my_start) % groups + groups * slot_ids).reshape(total_slots)
    other = swap_core(send)
    up, down = call(
        pack_x_kernel,
        None,
        [keep, other],
        [jax.ShapeDtypeStruct((3, *piece.shape[1:]), jnp.bfloat16)] * 2,
        [],
        keep.size,
        6 * keep.size,
    )

    def first_dot(beside, arrays, pieces, places):
        return call(
            functools.partial(first_kernel, pieces, share, qkv_width),
            places,
            [beside[0], cot_rows, *arrays],
            jax.ShapeDtypeStruct((row_count, width), jnp.float32),
            [],
            row_count * model_width * width,
            model_width * width,
        )

    early, late, begun, beside = gather_weights(
        call(
            join_kernel,
            None,
            [qkv_weight, out_weight],
            jax.ShapeDtypeStruct((share, width), jnp.bfloat16),
            [],
            share * width,
            4 * share * width,
        ),
        first_dot,
        (normed_b, keep, other, up, down, flag_cols, routing, position),
    )
    normed_b, keep, other, up, down, flag_cols, routing, position = beside
    slots = call(
        functools.partial(project_kernel, late[1], share, qkv_width),
        late[2],
        [normed_b, cot_rows, begun, routing, flag_cols, *late[0]],
        jax.ShapeDtypeStruct((total_slots, width + 128), jnp.bfloat16),
        [pltpu.VMEM((row_count, width), jnp.float32)],
        row_count * model_width * width,
        model_width * width,
    )
    blocks = [*early[0], *late[0]]
    pieces = early[1] + [(len(early[0]) + which, *rest) for which, *rest in late[1]]
    places = jnp.concatenate([early[2], late[2]])
    slots, keep, other, up, down = lax.optimization_barrier((slots, keep, other, up, down))
    got = swap_dp(slots.reshape(groups, slot_count, width + 128))
    cols, col_pieces = spread_cols(keep, other, up, down)
    got = got.reshape(total_slots, width + 128)
    both = call(
        functools.partial(attention_kernel, QH),
        my_length[None],
        [position[:, None], position[None, :], got],
        jax.ShapeDtypeStruct((total_slots, width), jnp.bfloat16),
        [],
        18 * total_slots * total_slots * out_width,
        4 * total_slots * width,
    )
    back = swap_dp(both.reshape(groups, slot_count, width))
    col_pieces = [
        (which, index, ((dc * 2 + dy) * 4 + dx) * row_count)
        for which, index, (dx, dy, dc) in col_pieces
    ]
    turned = call(
        functools.partial(turn_kernel, col_pieces),
        None,
        cols,
        jax.ShapeDtypeStruct((2 * share, owners * row_count), jnp.bfloat16),
        [],
        owners * row_count * share,
        8 * owners * row_count * share,
    )
    back, turned = lax.optimization_barrier((back, turned))
    both_rows = from_slots(back)
    row_blocks, row_pieces, row_slots = gather_rows(both_rows)
    each = -(-share * width // (128 * 8 * groups)) * 8
    partial = call(
        functools.partial(weight_grad_kernel, row_pieces, qkv_width),
        row_slots,
        [turned, *row_blocks],
        jax.ShapeDtypeStruct((groups * each, 128), jnp.bfloat16),
        [pltpu.VMEM((owners * row_count, width), jnp.bfloat16)],
        2 * owners * row_count * width * share,
        2 * owners * row_count * (width + 2 * share),
    )
    partial, both_late = lax.optimization_barrier((partial, both_rows))
    summed = sum_over_dp(partial.reshape(groups, each, 128))
    result, tokens_grad = call(
        functools.partial(finish_kernel, pieces, share, qkv_width),
        places,
        [both_late, token_rows, cot_rows, *blocks],
        [jax.ShapeDtypeStruct((row_count, model_width), jnp.bfloat16)] * 2,
        [pltpu.VMEM((row_count, model_width), jnp.float32)],
        2 * row_count * model_width * width,
        2 * model_width * width,
    )

    qkv_grad, out_grad = call(
        functools.partial(spread_kernel, qkv_width),
        None,
        [summed],
        [
            jax.ShapeDtypeStruct((share, qkv_width), jnp.float32),
            jax.ShapeDtypeStruct((share, out_width), jnp.float32),
        ],
        [],
        share * width,
        6 * share * width,
    )
    return (result[None, None], tokens_grad[None, None], qkv_grad, out_grad)


def swap_dp(array):
    return lax.all_to_all(array, DP, split_axis=0, concat_axis=0, tiled=True)


def sum_over_dp(partial):
    got = swap_dp(partial)
    mine = jnp.sum(got.astype(jnp.float32), axis=0).astype(jnp.bfloat16)
    return swap_dp(jnp.broadcast_to(mine[None], partial.shape)).reshape(-1, partial.shape[2])


def solution(mesh):
    fine = Mesh(mesh.devices.reshape(FINE), DP + FSDP)
    return jax.shard_map(
        on_device,
        mesh=fine,
        in_specs=(
            P(FSDP, DP, None, None),
            P(FSDP, DP, None, None),
            P(FSDP, None),
            P(FSDP, None),
            P(FSDP, None),
            P(FSDP, DP, None),
        ),
        out_specs=(
            P(FSDP, DP, None, None),
            P(FSDP, DP, None, None),
            P(FSDP, None),
            P(FSDP, None),
        ),
        check_vma=False,
    )
```
